256 devices in a mesh: lat: 64 (over z, y, x_hi), lon: 4 (over x_lo, core).
Axes of the slice: x: 4 (x_hi: 2, x_lo: 2; x = x_hi * 2 + x_lo), y: 4, z: 8, core: 2. Of those that a mesh axis runs over, the one named last changes fastest.
Arguments:
- grid_latent: bfloat16 [131072, 512], P(('lat', 'lon')), may hold values from -6 to 6
- grid_feat: bfloat16 [4, 524288], P(None, ('lat', 'lon')), may hold values from -6 to 6
- grid_sender: int32 [524288], P(('lat', 'lon')), may hold values from 0 to 511
- grid_owner: int32 [524288, 1], P(('lat', 'lon')), may hold values from 0 to 63; in each aligned block of 2048 rows (0 to 2047, 2048 to 4095, ...) at most 64 rows name the same one
- grid_node: int32 [524288], P(('lat', 'lon')), may hold values from 0 to 511
- mesh_latent: bfloat16 [32768, 512], P('lat', 'lon'), may hold values from -6 to 6
- mesh_edge: bfloat16 [262144, 512], P(('lat', 'lon')), may hold values from -6 to 6
- halo_send: int32 [4096, 8], P('lat'), may hold values from 0 to 511
- mesh_sender: int32 [262144], P(('lat', 'lon')), may hold values from 0 to 1023
- mesh_receiver: int32 [262144], P(('lat', 'lon')), may hold values from 0 to 511
- enc_edge_in: bfloat16 [512, 512], P(None, 'lon'), may hold values from -0.25 to 0.25
- enc_feat_proj: bfloat16 [4, 512], replicated, may hold values from -3 to 3
- enc_edge_out: bfloat16 [512, 512], P(None, 'lon'), may hold values from -0.25 to 0.25
- enc_edge_bias: float32 [2, 512], replicated, may hold values from -1.5 to 1.5
- enc_edge_gain: float32 [512], replicated, may hold values from 0.25 to 1.75
- enc_node_in: bfloat16 [1024, 512], P(None, 'lon'), may hold values from -0.1875 to 0.1875
- enc_node_out: bfloat16 [512, 512], P('lon'), may hold values from -0.25 to 0.25
- enc_node_bias: float32 [2, 512], replicated, may hold values from -1.5 to 1.5
- enc_node_gain: float32 [512], replicated, may hold values from 0.25 to 1.75
- proc_edge_in: bfloat16 [1536, 512], P(None, 'lon'), may hold values from -0.15625 to 0.15625
- proc_edge_out: bfloat16 [512, 512], P(None, 'lon'), may hold values from -0.25 to 0.25
- proc_edge_bias: float32 [2, 512], replicated, may hold values from -1.5 to 1.5
- proc_edge_gain: float32 [512], replicated, may hold values from 0.25 to 1.75
- proc_node_in: bfloat16 [1024, 512], P(None, 'lon'), may hold values from -0.1875 to 0.1875
- proc_node_out: bfloat16 [512, 512], P('lon'), may hold values from -0.25 to 0.25
- proc_node_bias: float32 [2, 512], replicated, may hold values from -1.5 to 1.5
- proc_node_gain: float32 [512], replicated, may hold values from 0.25 to 1.75
Outputs:
- mesh_update: bfloat16 [32768, 512], P('lat', 'lon')
- edge_update: bfloat16 [262144, 512], P(('lat', 'lon'))
The draws below stay inside these ranges and needn't reach their ends.
Inputs may be any that keep to these rules, and one draw needn't show every extreme that they name: `grid_sender`: a row among the 512 grid rows of the device that holds the edge. `grid_owner`: among the 2048 edges of one device, at most 64 name the same partition, a bound that some block reaches. `halo_send`: nodes of the listing partition.
All inputs are finite; a program needn't handle non-finite values.
Results may differ from the reference program's by a relative error of at most 0.017.
Values may be sent and summed in bfloat16 or wider, within the bound.
A program may use at most 128 MiB of HBM per device.

```python
import math
import jax
import jax.numpy as jnp
import numpy as np
from jax import lax

D = 512
EF = 4
DEG = 8
G_DEV = 512
MESH_DEV = 512
GE_DEV = 2048
CAP = 64
HCAP = 8
GRID = 131072
GRID_EDGES = 524288
MESH = 32768
MESH_EDGES = 262144
N_LAT = 64
N_LON = 4


def touch_ends(drawn, stream_key, least, high):
    extent = drawn.shape
    index_at = [jax.random.randint(jax.random.fold_in(stream_key, axis), (), 0, extent[axis]) for axis in range(len(extent))]
    drawn = drawn.at[tuple(index_at)].set(least)
    longest = extent.index(max(extent))
    index_at[longest] = (index_at[longest] + 1) % extent[longest]
    return drawn.at[tuple(index_at)].set(high)


def level_of(key, shape, shards, smallest, largest):
    level = 1.0
    for position, shards_of in shards:
        draws = jax.random.uniform(jax.random.fold_in(jax.random.fold_in(key, 6), position), (shards_of,), jnp.float32, smallest / len(shards), largest / len(shards))
        level = level * jnp.repeat(jnp.exp(draws), shape[position] // shards_of).reshape((-1,) + (1,) * (len(shape) - 1 - position))
    return level


def shared_out(rng, own, number, rows, number_of, top, limit, skew):
    sequence = jax.random.permutation(rng, number_of)
    crowded, usual = portions_of(number_of, rows * top, limit, skew, True), portions_of(number_of, rows * top, limit, skew, False)
    places = jnp.arange(number_of)

    def named(lengths, offset_by):
        used = int((lengths > 0).sum())
        fixed = max(1, used // 4)
        passed = fixed + (places - fixed + offset_by * (used - fixed)) % max(1, number_of - fixed)
        return jnp.zeros((number_of,), jnp.int32).at[sequence[jnp.where(places < fixed, places, passed)]].set(jnp.asarray(lengths, jnp.int32))

    lengths = jnp.where(number % 4 == 0, named(crowded, number // 4), named(usual, number - number // 4 - 1))
    mixed = jax.random.permutation(jax.random.fold_in(own, 3), number_of)
    donor, sink = mixed[0:number_of // 2 * 2:2], mixed[1:number_of // 2 * 2:2]
    margin = jnp.minimum(lengths[donor] - 1, limit - lengths[sink]) // 2
    margin = jnp.where((donor == sequence[0]) | (sink == sequence[0]) | (lengths[sink] == 0), 0, jnp.maximum(margin, 0))
    passed = jax.random.randint(jax.random.fold_in(own, 4), (number_of // 2,), 0, 1 << 20) % (margin + 1)
    lengths = lengths.at[donor].add(-passed).at[sink].add(passed)
    members = jnp.searchsorted(jnp.cumsum(lengths), jnp.arange(rows * top), side="right").astype(jnp.int32)
    grid = members.reshape(top, rows).T
    grid = grid[jax.random.permutation(jax.random.fold_in(own, 1), rows)]
    offset_by = jax.random.randint(jax.random.fold_in(own, 2), (rows, 1), 0, top)
    return jnp.take_along_axis(grid, (jnp.arange(top)[None, :] + offset_by) % top, axis=1)


def portions_of(count, total, bound, skew, full):
    loads = [(1 << 20) // math.isqrt(standing ** skew) + 1 for standing in range(1, count + 1)]
    largest = bound if full else min(bound, max(-(-total // count), total * loads[0] // sum(loads)))
    least = 1 if total - largest >= count - 1 else 0
    counts, spare = [largest] + [least] * (count - 1), total - largest - least * (count - 1)
    while spare > 0:
        free = [i for i in range(1, count) if counts[i] < largest] or [i for i in range(1, count) if counts[i] < bound]
        whole, budget = sum([loads[i] for i in free]), spare
        for i in free:
            extra = min(bound - counts[i], max(1, budget * loads[i] // whole), spare)
            counts[i] = counts[i] + extra
            spare = spare - extra
    return np.array(counts)


def scatter_about(own_key, shape, scale, bound, split=(), kind=jnp.bfloat16):
    entries = jax.random.normal(own_key, shape, jnp.float32) * scale
    if len(split) > 0:
        entries = level_of(own_key, shape, split, -0.22, 0.18) * entries
    return jnp.clip(entries, min=-bound, max=bound).astype(kind)


def setup_inputs(seed: int = 0) -> dict:
    streams_of = jax.random.split(jax.random.key(seed), 28)
    grid_latent = scatter_about(streams_of[0], (GRID, D), 1.0, 6.0, ((0, 256),))
    grid_feat = scatter_about(streams_of[1], (EF, GRID_EDGES), 1.0, 6.0, ((1, 256),))
    grid_sender = touch_ends(jax.random.randint(streams_of[2], (GRID_EDGES,), 0, G_DEV), jax.random.fold_in(streams_of[2], 1), 0, G_DEV - 1).astype(jnp.int32)
    grid_owner_keys = jax.random.split(jax.random.fold_in(streams_of[3], 1), GRID_EDGES // GE_DEV)
    grid_owner_turns = jax.random.permutation(jax.random.fold_in(streams_of[3], 3), GRID_EDGES // GE_DEV)
    grid_owner = jax.vmap(lambda own, number: shared_out(jax.random.fold_in(streams_of[3], 2), own, number, GE_DEV, N_LAT, 1, CAP, 2))(grid_owner_keys, grid_owner_turns).reshape((GRID_EDGES, 1))
    grid_node = touch_ends(jax.random.randint(streams_of[4], (GRID_EDGES,), 0, MESH_DEV), jax.random.fold_in(streams_of[4], 1), 0, MESH_DEV - 1).astype(jnp.int32)
    mesh_latent = scatter_about(streams_of[5], (MESH, D), 1.0, 6.0, ((0, 64), (1, 4)))
    mesh_edge = scatter_about(streams_of[6], (MESH_EDGES, D), 1.0, 6.0, ((0, 256),))
    halo_send = touch_ends(jax.random.randint(streams_of[7], (N_LAT * N_LAT, HCAP), 0, MESH_DEV), jax.random.fold_in(streams_of[7], 1), 0, MESH_DEV - 1).astype(jnp.int32)
    mesh_sender = touch_ends(jax.random.randint(streams_of[8], (MESH_EDGES,), 0, MESH_DEV + N_LAT * HCAP), jax.random.fold_in(streams_of[8], 1), 0, (MESH_DEV + N_LAT * HCAP) - 1).astype(jnp.int32)
    mesh_receiver = touch_ends(jax.random.randint(streams_of[9], (MESH_EDGES,), 0, MESH_DEV), jax.random.fold_in(streams_of[9], 1), 0, MESH_DEV - 1).astype(jnp.int32)
    enc_edge_in = scatter_about(streams_of[10], (D, D), D ** -0.5, 0.25, ((1, 4),))
    enc_feat_proj = scatter_about(streams_of[11], (EF, D), EF ** -0.5, 3.0)
    enc_edge_out = scatter_about(streams_of[12], (D, D), D ** -0.5, 0.25, ((1, 4),))
    enc_edge_bias = scatter_about(streams_of[13], (2, D), 0.3, 1.5, (), jnp.float32)
    enc_edge_gain = jnp.clip(1.0 + 0.15 * jax.random.normal(streams_of[14], (D,), jnp.float32), 0.25, 1.75)
    enc_node_in = scatter_about(streams_of[15], (2 * D, D), (2 * D) ** -0.5, 0.1875, ((1, 4),))
    enc_node_out = scatter_about(streams_of[16], (D, D), D ** -0.5, 0.25, ((0, 4),))
    enc_node_bias = scatter_about(streams_of[17], (2, D), 0.3, 1.5, (), jnp.float32)
    enc_node_gain = jnp.clip(1.0 + 0.15 * jax.random.normal(streams_of[18], (D,), jnp.float32), 0.25, 1.75)
    proc_edge_in = scatter_about(streams_of[19], (3 * D, D), (3 * D) ** -0.5, 0.15625, ((1, 4),))
    proc_edge_out = scatter_about(streams_of[20], (D, D), D ** -0.5, 0.25, ((1, 4),))
    proc_edge_bias = scatter_about(streams_of[21], (2, D), 0.3, 1.5, (), jnp.float32)
    proc_edge_gain = jnp.clip(1.0 + 0.15 * jax.random.normal(streams_of[22], (D,), jnp.float32), 0.25, 1.75)
    proc_node_in = scatter_about(streams_of[23], (2 * D, D), (2 * D) ** -0.5, 0.1875, ((1, 4),))
    proc_node_out = scatter_about(streams_of[24], (D, D), D ** -0.5, 0.25, ((0, 4),))
    proc_node_bias = scatter_about(streams_of[25], (2, D), 0.3, 1.5, (), jnp.float32)
    proc_node_gain = jnp.clip(1.0 + 0.15 * jax.random.normal(streams_of[26], (D,), jnp.float32), 0.25, 1.75)
    return {"grid_latent": grid_latent, "grid_feat": grid_feat, "grid_sender": grid_sender, "grid_owner": grid_owner, "grid_node": grid_node, "mesh_latent": mesh_latent, "mesh_edge": mesh_edge, "halo_send": halo_send, "mesh_sender": mesh_sender, "mesh_receiver": mesh_receiver, "enc_edge_in": enc_edge_in, "enc_feat_proj": enc_feat_proj, "enc_edge_out": enc_edge_out, "enc_edge_bias": enc_edge_bias, "enc_edge_gain": enc_edge_gain, "enc_node_in": enc_node_in, "enc_node_out": enc_node_out, "enc_node_bias": enc_node_bias, "enc_node_gain": enc_node_gain, "proc_edge_in": proc_edge_in, "proc_edge_out": proc_edge_out, "proc_edge_bias": proc_edge_bias, "proc_edge_gain": proc_edge_gain, "proc_node_in": proc_node_in, "proc_node_out": proc_node_out, "proc_node_bias": proc_node_bias, "proc_node_gain": proc_node_gain}


def layer_norm(values, norm_gain, offsets):
    average = lax.optimization_barrier(jnp.mean(values, axis=-1, keepdims=True))
    centred = values - average
    spread = lax.optimization_barrier(jnp.mean(centred * centred, axis=-1, keepdims=True))
    return centred * lax.rsqrt(spread + 1e-05) * norm_gain + offsets

def node_network(base, aggregate, weight_in, weight_out, biases, norm_gain):
    inputs = jnp.concatenate([base, aggregate], 1)
    hidden = jax.nn.silu(jnp.dot(inputs, weight_in, preferred_element_type=jnp.float32) + biases[0]).astype(jnp.bfloat16)
    raw_out = jnp.dot(hidden, weight_out, preferred_element_type=jnp.float32)
    return (base.astype(jnp.float32) + layer_norm(raw_out, norm_gain, biases[1])).astype(jnp.bfloat16)

def reference(grid_latent, grid_feat, grid_sender, grid_owner, grid_node, mesh_latent, mesh_edge, halo_send, mesh_sender, mesh_receiver, enc_edge_in, enc_feat_proj, enc_edge_out, enc_edge_bias, enc_edge_gain, enc_node_in, enc_node_out, enc_node_bias, enc_node_gain, proc_edge_in, proc_edge_out, proc_edge_bias, proc_edge_gain, proc_node_in, proc_node_out, proc_node_bias, proc_node_gain):
    device_count = N_LAT * N_LON
    mesh_count = MESH_DEV * N_LAT
    owner_column = grid_owner[:, 0]

    def encode(summed, device):
        first = device * GE_DEV
        senders = lax.dynamic_slice_in_dim(grid_sender, first, GE_DEV) + device * G_DEV
        source_rows = jnp.take(grid_latent, senders, axis=0)
        feats = lax.dynamic_slice_in_dim(grid_feat, first, GE_DEV, 1)
        feat_term = jnp.dot(feats.T, enc_feat_proj, preferred_element_type=jnp.float32) + enc_edge_bias[0]
        pre_act = jnp.dot(source_rows, enc_edge_in, preferred_element_type=jnp.float32) + feat_term
        hidden = jax.nn.silu(pre_act).astype(jnp.bfloat16)
        raw_out = jnp.dot(hidden, enc_edge_out.T, preferred_element_type=jnp.float32)
        messages = layer_norm(raw_out, enc_edge_gain, enc_edge_bias[1])
        owners = lax.dynamic_slice_in_dim(owner_column, first, GE_DEV)
        nodes = lax.dynamic_slice_in_dim(grid_node, first, GE_DEV)
        return (summed.at[owners * MESH_DEV + nodes].add(messages), device)
    start_sum = jnp.zeros((mesh_count, D), jnp.float32)
    gathered, leftover = lax.scan(encode, start_sum, jnp.arange(device_count, dtype=jnp.int32))
    mesh_mid = node_network(mesh_latent, gathered.astype(jnp.bfloat16), enc_node_in, enc_node_out, enc_node_bias, enc_node_gain)
    halo_table = halo_send.reshape(N_LAT, N_LAT, HCAP)
    part_edges = MESH_DEV * DEG

    def process(part):
        local = lax.dynamic_slice_in_dim(mesh_mid, part * MESH_DEV, MESH_DEV)
        picks = lax.dynamic_index_in_dim(halo_table, part, 1, keepdims=False)
        global_rows = (jnp.arange(N_LAT, dtype=jnp.int32)[:, None] * MESH_DEV + picks).reshape(-1)
        table = jnp.concatenate([local, jnp.take(mesh_mid, global_rows, axis=0)], 0)
        first = part * part_edges
        edges = lax.dynamic_slice_in_dim(mesh_edge, first, part_edges)
        senders = lax.dynamic_slice_in_dim(mesh_sender, first, part_edges)
        receivers = lax.dynamic_slice_in_dim(mesh_receiver, first, part_edges)
        sender_rows = jnp.take(table, senders, axis=0)
        receiver_rows = jnp.take(local, receivers, axis=0)
        pre_act = jnp.dot(edges, proc_edge_in[:D], preferred_element_type=jnp.float32)
        pre_act = pre_act + jnp.dot(sender_rows, proc_edge_in[D:2 * D], preferred_element_type=jnp.float32)
        pre_act = pre_act + jnp.dot(receiver_rows, proc_edge_in[2 * D:], preferred_element_type=jnp.float32)
        hidden = jax.nn.silu(pre_act + proc_edge_bias[0]).astype(jnp.bfloat16)
        raw_out = jnp.dot(hidden, proc_edge_out.T, preferred_element_type=jnp.float32)
        updated = (edges.astype(jnp.float32) + layer_norm(raw_out, proc_edge_gain, proc_edge_bias[1])).astype(jnp.bfloat16)
        onehot = (jnp.arange(MESH_DEV, dtype=jnp.int32)[:, None] == receivers[None, :]).astype(jnp.bfloat16)
        incoming = jnp.dot(onehot, updated, preferred_element_type=jnp.float32)
        return (updated, incoming)
    edge_blocks, incoming_blocks = lax.map(process, jnp.arange(N_LAT, dtype=jnp.int32))
    edge_update = edge_blocks.reshape(-1, D)
    incoming = incoming_blocks.reshape(-1, D)
    mesh_update = node_network(mesh_mid, incoming.astype(jnp.bfloat16), proc_node_in, proc_node_out, proc_node_bias, proc_node_gain)
    return (mesh_update, edge_update)
```

```python
import jax
import jax.numpy as jnp
from jax import lax
from jax.experimental import pallas as pl
from jax.experimental.pallas import tpu as pltpu
from jax.sharding import PartitionSpec as P

F32 = jnp.float32
BF16 = jnp.bfloat16
LAT = 64
LON = 4
WIDTH = 512
NODES = 512
CAP = 64
ROWS = NODES // LON


def matmul(a, b):
    return jnp.dot(a, b, preferred_element_type=F32)


def matmul_t(a, b):
    return lax.dot_general(a, b, (((0,), (0,)), ((), ())), preferred_element_type=F32)


def matmul_nt(a, b):
    return lax.dot_general(a, b, (((1,), (1,)), ((), ())), preferred_element_type=F32)


def swish(t):
    return t / (1.0 + jnp.exp(-t))


def layer_norm(values, gain, offset):
    average = jnp.mean(values, axis=-1, keepdims=True)
    centred = values - average
    spread = jnp.mean(centred * centred, axis=-1, keepdims=True)
    return centred * lax.rsqrt(spread + 1e-05) * gain + offset


def one_hot(row, count):
    width = row.shape[1]
    return (lax.broadcasted_iota(jnp.int32, (count, width), 0) == row).astype(BF16)


def slot_fields(owners, sender, node, feat):
    count = owners.shape[0]
    block = 128
    hit = (owners[:, None] == jnp.arange(LAT, dtype=jnp.int32)[None, :]).astype(BF16)
    blocks = hit.reshape(count // block, block, LAT)
    below = jnp.tril(jnp.ones((block, block), BF16), -1)
    inside = jnp.einsum("ij,bjk->bik", below, blocks, preferred_element_type=F32)
    totals = jnp.sum(blocks.astype(F32), axis=1)
    earlier = jnp.tril(jnp.ones((count // block, count // block), F32), -1)
    before = jnp.sum(earlier[:, :, None] * totals[None], axis=1)
    rank = jnp.sum((inside + before[:, None, :]) * blocks.astype(F32), axis=2).reshape(count)
    place = (rank.astype(jnp.int32)[:, None] == jnp.arange(CAP, dtype=jnp.int32)[None, :]).astype(BF16)
    shifted = node + 1
    values = [sender >> 8, sender & 255, shifted >> 8, shifted & 255]
    values = [v.astype(BF16) for v in values] + [feat[i] for i in range(4)]
    spread = jnp.concatenate([place * v[:, None] for v in values], axis=1)
    slots = matmul_t(hit, spread).reshape(LAT, 8, CAP)
    return jnp.moveaxis(slots, 1, 0).reshape(8, LAT * CAP)


def encoder_kernel(step, sender, feat, grid, w_in, proj, w_out, bias, gain, out):
    rows = matmul_t(one_hot(sender[...], WIDTH), grid[...]).astype(BF16)
    pre = matmul(rows, w_in[...]) + (matmul_t(feat[...], proj[...]) + bias[0:1, :])
    hidden = swish(pre).astype(BF16)
    raw = matmul_nt(hidden, w_out[...])
    out[...] = layer_norm(raw, gain[...], bias[1:2, :]).astype(BF16)


def encode(sender, feat, grid, w_in, proj, w_out, bias, gain):
    total = sender.shape[1]
    step = 256
    whole = lambda i: (0, 0)
    return pl.pallas_call(
        lambda *refs: encoder_kernel(step, *refs),
        grid=(total // step,),
        in_specs=[
            pl.BlockSpec((1, step), lambda i: (0, i)),
            pl.BlockSpec((8, step), lambda i: (0, i)),
            pl.BlockSpec((512, WIDTH), whole),
            pl.BlockSpec((WIDTH, WIDTH), whole),
            pl.BlockSpec((8, WIDTH), whole),
            pl.BlockSpec((WIDTH, WIDTH), whole),
            pl.BlockSpec((2, WIDTH), whole),
            pl.BlockSpec((1, WIDTH), whole),
        ],
        out_specs=pl.BlockSpec((step, WIDTH), lambda i: (i, 0)),
        out_shape=jax.ShapeDtypeStruct((total, WIDTH), BF16),
        name="encode",
    )(sender, feat, grid, w_in, proj, w_out, bias, gain)


def segment_kernel(ids, rows, out, acc):
    @pl.when(pl.program_id(0) == 0)
    def _():
        acc[...] = jnp.zeros_like(acc)

    acc[...] += matmul(one_hot(ids[...], NODES), rows[...])

    @pl.when(pl.program_id(0) == pl.num_programs(0) - 1)
    def _():
        out[...] = acc[...].astype(BF16)


def segment_sum(ids, rows):
    total = rows.shape[0]
    step = 512
    return pl.pallas_call(
        segment_kernel,
        grid=(total // step,),
        in_specs=[
            pl.BlockSpec((1, step), lambda i: (0, i)),
            pl.BlockSpec((step, WIDTH), lambda i: (i, 0)),
        ],
        out_specs=pl.BlockSpec((NODES, WIDTH), lambda i: (0, 0)),
        out_shape=jax.ShapeDtypeStruct((NODES, WIDTH), BF16),
        scratch_shapes=[pltpu.VMEM((NODES, WIDTH), F32)],
        name="segment",
    )(ids, rows)


def node_kernel(base, parts, w_in, w_out, bias, gain, out):
    summed = parts[0].astype(F32)
    for i in range(1, LON):
        summed = summed + parts[i].astype(F32)
    aggregate = summed.astype(BF16)
    pre = matmul(base[...], w_in[:WIDTH, :]) + matmul(aggregate, w_in[WIDTH:, :]) + bias[0:1, :]
    hidden = swish(pre).astype(BF16)
    raw = matmul(hidden, w_out[...])
    out[...] = (base[...].astype(F32) + layer_norm(raw, gain[...], bias[1:2, :])).astype(BF16)


def node_network(base, parts, w_in, w_out, bias, gain):
    return pl.pallas_call(
        node_kernel, out_shape=jax.ShapeDtypeStruct(base.shape, BF16), name="node"
    )(base, parts, w_in, w_out, bias, gain)


def edge_kernel(sender, receiver, edges, local, halo, w_in, w_out, bias, gain, out, partial, acc):
    @pl.when(pl.program_id(0) == 0)
    def _():
        acc[...] = jnp.zeros_like(acc)

    towards = one_hot(receiver[...], NODES)
    sent = matmul_t(one_hot(sender[...], NODES), local[...])
    sent = sent + matmul_t(one_hot(sender[...] - NODES, NODES), halo[...])
    got = matmul_t(towards, local[...])
    pre = matmul(edges[...], w_in[:WIDTH, :])
    pre = pre + matmul(sent.astype(BF16), w_in[WIDTH : 2 * WIDTH, :])
    pre = pre + matmul(got.astype(BF16), w_in[2 * WIDTH :, :])
    hidden = swish(pre + bias[0:1, :]).astype(BF16)
    raw = matmul_nt(hidden, w_out[...])
    updated = (edges[...].astype(F32) + layer_norm(raw, gain[...], bias[1:2, :])).astype(BF16)
    out[...] = updated
    acc[...] += matmul(towards, updated)

    @pl.when(pl.program_id(0) == pl.num_programs(0) - 1)
    def _():
        partial[...] = acc[...].astype(BF16)


def edge_network(sender, receiver, edges, local, halo, w_in, w_out, bias, gain):
    total = edges.shape[0]
    step = 256
    whole = lambda i: (0, 0)
    return pl.pallas_call(
        edge_kernel,
        grid=(total // step,),
        in_specs=[
            pl.BlockSpec((1, step), lambda i: (0, i)),
            pl.BlockSpec((1, step), lambda i: (0, i)),
            pl.BlockSpec((step, WIDTH), lambda i: (i, 0)),
            pl.BlockSpec((NODES, WIDTH), whole),
            pl.BlockSpec((NODES, WIDTH), whole),
            pl.BlockSpec((3 * WIDTH, WIDTH), whole),
            pl.BlockSpec((WIDTH, WIDTH), whole),
            pl.BlockSpec((2, WIDTH), whole),
            pl.BlockSpec((1, WIDTH), whole),
        ],
        out_specs=[
            pl.BlockSpec((step, WIDTH), lambda i: (i, 0)),
            pl.BlockSpec((NODES, WIDTH), whole),
        ],
        out_shape=[
            jax.ShapeDtypeStruct((total, WIDTH), BF16),
            jax.ShapeDtypeStruct((NODES, WIDTH), BF16),
        ],
        scratch_shapes=[pltpu.VMEM((NODES, WIDTH), F32)],
        name="edges",
    )(sender, receiver, edges, local, halo, w_in, w_out, bias, gain)


def swap(tiles, axis):
    return lax.all_to_all(tiles, axis, split_axis=0, concat_axis=0, tiled=True)


def local(
    grid_latent,
    grid_feat,
    grid_sender,
    grid_owner,
    grid_node,
    mesh_latent,
    mesh_edge,
    halo_send,
    mesh_sender,
    mesh_receiver,
    enc_edge_in,
    enc_feat_proj,
    enc_edge_out,
    enc_edge_bias,
    enc_edge_gain,
    enc_node_in,
    enc_node_out,
    enc_node_bias,
    enc_node_gain,
    proc_edge_in,
    proc_edge_out,
    proc_edge_bias,
    proc_edge_gain,
    proc_node_in,
    proc_node_out,
    proc_node_bias,
    proc_node_gain,
):
    first = lax.all_gather(
        jnp.concatenate([enc_edge_in, enc_edge_out], 0), "lon", axis=1, tiled=True
    )
    inner = lax.all_gather(
        jnp.concatenate([enc_node_in, proc_edge_in, proc_edge_out, proc_node_in], 0),
        "lon",
        axis=1,
        tiled=True,
    )
    outer = lax.all_gather(
        jnp.concatenate([enc_node_out, proc_node_out], 1), "lon", axis=0, tiled=True
    )
    base = swap(mesh_latent.reshape(LON, ROWS, ROWS), "lon")
    base = jnp.moveaxis(base, 0, 1).reshape(ROWS, WIDTH)

    fields = slot_fields(grid_owner[:, 0], grid_sender, grid_node, grid_feat)
    whole = fields[:4].astype(jnp.int32)
    sender = (whole[0] * 256 + whole[1]).reshape(1, -1)
    node = (whole[2] * 256 + whole[3] - 1).reshape(LAT, 1, CAP)
    feat = jnp.concatenate([fields[4:], jnp.zeros((4, LAT * CAP), F32)], 0).astype(BF16)
    proj = jnp.concatenate([enc_feat_proj, jnp.zeros((4, WIDTH), BF16)], 0)
    ids = swap(node, "lat")
    messages = encode(
        sender, feat, grid_latent, first[:WIDTH], proj, first[WIDTH:], enc_edge_bias, enc_edge_gain[None]
    )
    arrived = swap(messages.reshape(LAT, CAP, WIDTH), "lat").reshape(LAT * CAP, WIDTH)
    partial = segment_sum(ids.reshape(1, LAT * CAP), arrived)
    parts = swap(partial.reshape(LON, ROWS, WIDTH), "lon")
    middle = node_network(
        base, parts, inner[:1024], outer[:, :WIDTH], enc_node_bias, enc_node_gain[None]
    )
    mesh_mid = lax.all_gather(middle, "lon", axis=0, tiled=True)
    halo = swap(mesh_mid[halo_send], "lat").reshape(NODES, WIDTH)
    edge_update, partial = edge_network(
        mesh_sender.reshape(1, -1),
        mesh_receiver.reshape(1, -1),
        mesh_edge,
        mesh_mid,
        halo,
        inner[1024:2560],
        inner[2560:3072],
        proc_edge_bias,
        proc_edge_gain[None],
    )
    parts = swap(partial.reshape(LON, ROWS, WIDTH), "lon")
    newest = node_network(
        middle, parts, inner[3072:], outer[:, WIDTH:], proc_node_bias, proc_node_gain[None]
    )
    tiles = jnp.moveaxis(newest.reshape(ROWS, LON, ROWS), 1, 0)
    mesh_update = swap(tiles, "lon").reshape(NODES, ROWS)
    return (mesh_update, edge_update)


def solution(mesh):
    placed = (
        P(("lat", "lon"), None),
        P(None, ("lat", "lon")),
        P(("lat", "lon")),
        P(("lat", "lon"), None),
        P(("lat", "lon")),
        P("lat", "lon"),
        P(("lat", "lon"), None),
        P("lat", None),
        P(("lat", "lon")),
        P(("lat", "lon")),
        P(None, "lon"),
        P(),
        P(None, "lon"),
        P(),
        P(),
        P(None, "lon"),
        P("lon", None),
        P(),
        P(),
        P(None, "lon"),
        P(None, "lon"),
        P(),
        P(),
        P(None, "lon"),
        P("lon", None),
        P(),
        P(),
    )
    return jax.shard_map(
        local,
        mesh=mesh,
        in_specs=placed,
        out_specs=(P("lat", "lon"), P(("lat", "lon"), None)),
        check_vma=False,
    )
```

```python
import jax
import jax.numpy as jnp
from jax import lax
from jax.experimental import pallas as pl
from jax.experimental.pallas import tpu as pltpu
from jax.sharding import PartitionSpec as P

F32 = jnp.float32
BF16 = jnp.bfloat16
LAT = 64
LON = 4
WIDTH = 512
NODES = 512
CAP = 64
ROWS = NODES // LON
PLANE = 32
DEPTH = 8
MESH = pl.DeviceIdType.MESH


def matmul(a, b):
    return jnp.dot(a, b, preferred_element_type=F32)


def matmul_t(a, b):
    return lax.dot_general(a, b, (((0,), (0,)), ((), ())), preferred_element_type=F32)


def matmul_nt(a, b):
    return lax.dot_general(a, b, (((1,), (1,)), ((), ())), preferred_element_type=F32)


def swish(t):
    return t / (1.0 + jnp.exp(-t))


def layer_norm(values, gain, offset):
    average = jnp.mean(values, axis=-1, keepdims=True)
    centred = values - average
    spread = jnp.mean(centred * centred, axis=-1, keepdims=True)
    return centred * lax.rsqrt(spread + 1e-05) * gain + offset


def one_hot(row, count):
    width = row.shape[1]
    return (lax.broadcasted_iota(jnp.int32, (count, width), 0) == row).astype(BF16)


def slots_kernel(owner, sender, node, feat, idx, fields):
    count = owner.shape[1]
    block = 128
    owners = owner[...]
    hit = one_hot(owners, LAT)
    row = lax.broadcasted_iota(jnp.int32, (block, block), 0)
    column = lax.broadcasted_iota(jnp.int32, (block, block), 1)
    above = (row < column).astype(BF16)
    carry = jnp.zeros((LAT, 1), F32)
    ranks = []
    for at in range(0, count, block):
        part = hit[:, at : at + block]
        wide = part.astype(F32)
        before = matmul(part, above) + carry
        ranks.append(jnp.sum(before * wide, axis=0, keepdims=True))
        carry = carry + jnp.sum(wide, axis=1, keepdims=True)
    rank = jnp.concatenate(ranks, axis=1).astype(jnp.int32)
    half = owners // 32
    target = (owners % 8) * 4 + (owners // 8) % 4
    at_target = one_hot(target, PLANE)
    place = one_hot(rank + half * CAP, 2 * CAP).astype(F32)
    named = node[...] + half * NODES + 1

    def put(values):
        return matmul_nt(at_target, (place * values.astype(F32)).astype(BF16))

    def put_whole(values):
        return (put(values // 32) * 32.0 + put(values % 32)).astype(jnp.int32)

    idx[:, :128] = put_whole(sender[...])
    idx[:, 128:] = put_whole(named) - 1
    for i in range(4):
        fields[:, i * 128 : (i + 1) * 128] = put(feat[i : i + 1, :])
    fields[:, 512:] = jnp.zeros((PLANE, 512), F32)


def slots(owner, sender, node, feat):
    return pl.pallas_call(
        slots_kernel,
        out_shape=[
            jax.ShapeDtypeStruct((PLANE, 256), jnp.int32),
            jax.ShapeDtypeStruct((PLANE, 1024), F32),
        ],
        name="slots",
    )(owner, sender, node, feat)


def remote(source, target, send, receive, where):
    return pltpu.make_async_remote_copy(
        src_ref=source,
        dst_ref=target,
        send_sem=send,
        recv_sem=receive,
        device_id=where,
        device_id_type=MESH,
    )


def gather_kernel(
    idx, feat, grid, w_in, proj, w_out, bias, gain, mesh, node_in, node_out, node_bias, node_gain,
    out,
    send, got, got_ids, acc, part, plane, share, aggregate, base, middle, whole,
    s_msg, r_msg, s_ids, r_ids, s_z, r_z, s_share, r_share, s_base, r_base, s_mid, r_mid,
):
    lat = lax.axis_index("lat")
    lon = lax.axis_index("lon")
    z = lat // 8
    cell = lat % 8
    place = cell * LON + lon
    owner = z % 4 == lon

    def at_place(t):
        return {"lat": z * 8 + t // LON, "lon": t % LON}

    def at_depth(depth):
        return {"lat": depth * 8 + cell, "lon": lon}

    def beside(step):
        return {"lat": lat, "lon": (lon + step) % LON}

    barrier = pltpu.get_barrier_semaphore()

    def greet(d, _):
        pl.semaphore_signal(barrier, inc=1, device_id=at_place((place + d) % PLANE), device_id_type=MESH)
        return 0

    lax.fori_loop(1, PLANE, greet, 0)

    @pl.when(owner)
    def _():
        def greet_all(d, _):
            pl.semaphore_signal(barrier, inc=1, device_id=at_depth((z + d) % DEPTH), device_id_type=MESH)
            return 0

        lax.fori_loop(1, DEPTH, greet_all, 0)

    @pl.when(z % 4 != lon)
    def _():
        pl.semaphore_signal(barrier, inc=1, device_id=at_depth(lon), device_id_type=MESH)
        pl.semaphore_signal(barrier, inc=1, device_id=at_depth(lon + 4), device_id_type=MESH)

    def target(d):
        return (place + d) % PLANE

    def compute(d):
        one, two = target(d), target(d + 1)
        sender = jnp.concatenate([idx[one][0:1, :], idx[two][0:1, :]], axis=1)
        features = jnp.concatenate([feat[one], feat[two]], axis=1).astype(BF16)
        rows = matmul_t(one_hot(sender, WIDTH), grid[...]).astype(BF16)
        pre = matmul(rows, w_in[...]) + (matmul_t(features, proj[...]) + bias[0:1, :])
        raw = matmul_nt(swish(pre).astype(BF16), w_out[...])
        message = layer_norm(raw, gain[...], bias[1:2, :]).astype(BF16)
        send[d] = message[:128]
        send[d + 1] = message[128:]

    def message_copy(d):
        return remote(send.at[d], got.at[d], s_msg.at[d], r_msg.at[d], at_place(target(d)))

    def ids_copy(d):
        return remote(idx.at[target(d)], got_ids.at[d], s_ids.at[d], r_ids.at[d], at_place(target(d)))

    def base_copy(step):
        other = (lon + step) % LON
        return remote(
            mesh.at[pl.ds(pl.multiple_of(other * ROWS, ROWS), ROWS), :],
            base.at[:, pl.ds(pl.multiple_of(lon * ROWS, ROWS), ROWS)],
            s_base.at[step],
            r_base.at[step],
            beside(step),
        )

    def base_arrival(step):
        other = (lon - step + LON) % LON
        return remote(
            mesh.at[pl.ds(0, ROWS), :],
            base.at[:, pl.ds(pl.multiple_of(other * ROWS, ROWS), ROWS)],
            s_base.at[step],
            r_base.at[step],
            beside(step),
        )

    compute(0)
    got[0] = send[0]
    got_ids[0] = idx[place]

    @pl.when(owner)
    def _():
        pl.semaphore_wait(barrier, PLANE - 1 + DEPTH - 1)

    @pl.when(z % 4 != lon)
    def _():
        pl.semaphore_wait(barrier, PLANE - 1 + 2)

    message_copy(1).start()

    def start_ids(d, _):
        ids_copy(d).start()
        return 0

    lax.fori_loop(1, PLANE, start_ids, 0)

    def start_messages(s, _):
        compute(2 * s)
        message_copy(2 * s).start()
        message_copy(2 * s + 1).start()
        return 0

    lax.fori_loop(1, PLANE // 2, start_messages, 0)
    for step in range(1, LON):
        base_copy(step).start()
    mine = pl.ds(pl.multiple_of(lon * ROWS, ROWS), ROWS)
    base[:, mine] = mesh[mine, :]

    acc[...] = jnp.zeros_like(acc)

    def take(g):
        ids = jnp.concatenate([got_ids[4 * g + i][1:2, :] for i in range(4)], axis=1)
        rows = jnp.concatenate([got[4 * g + i] for i in range(4)], axis=0)
        acc[...] += matmul(one_hot(ids, 2 * NODES), rows)

    def arrive(d):
        ids_copy(d).wait_recv()
        message_copy(d).wait_recv()

    for d in range(1, 4):
        arrive(d)
    take(0)

    def collect(g, _):
        for i in range(4):
            arrive(4 * g + i)
        take(g)
        return 0

    lax.fori_loop(1, PLANE // 4, collect, 0)

    def depth_copy(j, q):
        depth = lon + 4 * j
        away = (depth - z + DEPTH) % DEPTH
        return remote(
            part.at[pl.ds(j * NODES + q * ROWS, ROWS), :],
            plane.at[away, pl.ds(q * ROWS, ROWS), :],
            s_z.at[j, q],
            r_z.at[away, q],
            at_depth(depth),
        )

    for q in range(LON):
        for j in range(2):
            rows = pl.ds(j * NODES + q * ROWS, ROWS)
            part[rows, :] = acc[rows, :].astype(BF16)

            @pl.when(z != lon + 4 * j)
            def _():
                depth_copy(j, q).start()

    def share_copy(q):
        return remote(share.at[q], aggregate, s_share.at[q], r_share.at[0], {"lat": lat, "lon": q})

    @pl.when(owner)
    def _():
        for q in range(LON):
            first = pl.multiple_of((z // 4) * NODES + q * ROWS, ROWS)
            total = acc[pl.ds(first, ROWS), :]
            for away in range(1, DEPTH):
                remote(
                    part.at[pl.ds(0, ROWS), :],
                    plane.at[away, pl.ds(q * ROWS, ROWS), :],
                    s_z.at[0, q],
                    r_z.at[away, q],
                    at_depth(z),
                ).wait_recv()
                total = total + plane[away, pl.ds(q * ROWS, ROWS), :].astype(F32)
            rounded = total.astype(BF16)

            @pl.when(lon == q)
            def _():
                aggregate[...] = rounded

            @pl.when(lon != q)
            def _():
                share[q] = rounded
                share_copy(q).start()

    for step in range(1, LON):
        base_arrival(step).wait_recv()
    before = base[...]
    pre_base = matmul(before, node_in[:WIDTH, :])

    @pl.when(z % 4 != lon)
    def _():
        share_copy(0).wait_recv()

    pre = pre_base + matmul(aggregate[...], node_in[WIDTH:, :]) + node_bias[0:1, :]
    raw = matmul(swish(pre).astype(BF16), node_out[...])
    updated = before.astype(F32) + layer_norm(raw, node_gain[...], node_bias[1:2, :])
    middle[...] = updated.astype(BF16)

    def middle_copy(step):
        return remote(
            middle,
            whole.at[pl.ds(pl.multiple_of(lon * ROWS, ROWS), ROWS), :],
            s_mid.at[step],
            r_mid.at[step],
            beside(step),
        )

    def middle_arrival(step):
        other = (lon - step + LON) % LON
        return remote(
            middle,
            whole.at[pl.ds(pl.multiple_of(other * ROWS, ROWS), ROWS), :],
            s_mid.at[step],
            r_mid.at[step],
            beside(step),
        )

    for step in range(1, LON):
        middle_copy(step).start()
    whole[mine, :] = middle[...]
    for step in range(1, LON):
        middle_arrival(step).wait_recv()
    out[...] = whole[...]

    def sent(d, _):
        ids_copy(d).wait_send()
        message_copy(d).wait_send()
        return 0

    lax.fori_loop(1, PLANE, sent, 0)
    for step in range(1, LON):
        base_copy(step).wait_send()
        middle_copy(step).wait_send()
    for q in range(LON):
        for j in range(2):

            @pl.when(z != lon + 4 * j)
            def _():
                depth_copy(j, q).wait_send()

    @pl.when(owner)
    def _():
        for q in range(LON):

            @pl.when(lon != q)
            def _():
                share_copy(q).wait_send()


def gather_nodes(*operands):
    dma = pltpu.SemaphoreType.DMA
    return pl.pallas_call(
        gather_kernel,
        in_specs=[pl.BlockSpec(memory_space=pltpu.VMEM)] * len(operands),
        out_specs=pl.BlockSpec(memory_space=pltpu.VMEM),
        out_shape=jax.ShapeDtypeStruct((NODES, WIDTH), BF16),
        scratch_shapes=[
            pltpu.VMEM((PLANE, 128, WIDTH), BF16),
            pltpu.VMEM((PLANE, 128, WIDTH), BF16),
            pltpu.VMEM((PLANE, 2, 128), jnp.int32),
            pltpu.VMEM((2 * NODES, WIDTH), F32),
            pltpu.VMEM((2 * NODES, WIDTH), BF16),
            pltpu.VMEM((DEPTH, NODES, WIDTH), BF16),
            pltpu.VMEM((LON, ROWS, WIDTH), BF16),
            pltpu.VMEM((ROWS, WIDTH), BF16),
            pltpu.VMEM((ROWS, WIDTH), BF16),
            pltpu.VMEM((ROWS, WIDTH), BF16),
            pltpu.VMEM((NODES, WIDTH), BF16),
            dma((PLANE,)),
            dma((PLANE,)),
            dma((PLANE,)),
            dma((PLANE,)),
            dma((2, LON)),
            dma((DEPTH, LON)),
            dma((LON,)),
            dma((1,)),
            dma((LON,)),
            dma((LON,)),
            dma((LON,)),
            dma((LON,)),
        ],
        compiler_params=pltpu.CompilerParams(collective_id=0, has_side_effects=True),
        name="gather_nodes",
    )(*operands)


def node_kernel(base, parts, w_in, w_out, bias, gain, out):
    summed = parts[0].astype(F32)
    for i in range(1, LON):
        summed = summed + parts[i].astype(F32)
    aggregate = summed.astype(BF16)
    pre = matmul(base[...], w_in[:WIDTH, :]) + matmul(aggregate, w_in[WIDTH:, :]) + bias[0:1, :]
    hidden = swish(pre).astype(BF16)
    raw = matmul(hidden, w_out[...])
    out[...] = (base[...].astype(F32) + layer_norm(raw, gain[...], bias[1:2, :])).astype(BF16)


def node_network(base, parts, w_in, w_out, bias, gain):
    return pl.pallas_call(
        node_kernel, out_shape=jax.ShapeDtypeStruct(base.shape, BF16), name="node"
    )(base, parts, w_in, w_out, bias, gain)


def edge_kernel(sender, receiver, edges, local, halo, w_in, w_out, bias, gain, out, partial, acc):
    @pl.when(pl.program_id(0) == 0)
    def _():
        acc[...] = jnp.zeros_like(acc)

    towards = one_hot(receiver[...], NODES)
    sent = matmul_t(one_hot(sender[...], NODES), local[...])
    sent = sent + matmul_t(one_hot(sender[...] - NODES, NODES), halo[...])
    got = matmul_t(towards, local[...])
    pre = matmul(edges[...], w_in[:WIDTH, :])
    pre = pre + matmul(sent.astype(BF16), w_in[WIDTH : 2 * WIDTH, :])
    pre = pre + matmul(got.astype(BF16), w_in[2 * WIDTH :, :])
    hidden = swish(pre + bias[0:1, :]).astype(BF16)
    raw = matmul_nt(hidden, w_out[...])
    updated = (edges[...].astype(F32) + layer_norm(raw, gain[...], bias[1:2, :])).astype(BF16)
    out[...] = updated
    acc[...] += matmul(towards, updated)

    @pl.when(pl.program_id(0) == pl.num_programs(0) - 1)
    def _():
        partial[...] = acc[...].astype(BF16)


def edge_network(sender, receiver, edges, local, halo, w_in, w_out, bias, gain):
    total = edges.shape[0]
    step = 256
    whole = lambda i: (0, 0)
    return pl.pallas_call(
        edge_kernel,
        grid=(total // step,),
        in_specs=[
            pl.BlockSpec((1, step), lambda i: (0, i)),
            pl.BlockSpec((1, step), lambda i: (0, i)),
            pl.BlockSpec((step, WIDTH), lambda i: (i, 0)),
            pl.BlockSpec((NODES, WIDTH), whole),
            pl.BlockSpec((NODES, WIDTH), whole),
            pl.BlockSpec((3 * WIDTH, WIDTH), whole),
            pl.BlockSpec((WIDTH, WIDTH), whole),
            pl.BlockSpec((2, WIDTH), whole),
            pl.BlockSpec((1, WIDTH), whole),
        ],
        out_specs=[
            pl.BlockSpec((step, WIDTH), lambda i: (i, 0)),
            pl.BlockSpec((NODES, WIDTH), whole),
        ],
        out_shape=[
            jax.ShapeDtypeStruct((total, WIDTH), BF16),
            jax.ShapeDtypeStruct((NODES, WIDTH), BF16),
        ],
        scratch_shapes=[pltpu.VMEM((NODES, WIDTH), F32)],
        name="edges",
    )(sender, receiver, edges, local, halo, w_in, w_out, bias, gain)


def swap(tiles, axis):
    return lax.all_to_all(tiles, axis, split_axis=0, concat_axis=0, tiled=True)


def local(
    grid_latent,
    grid_feat,
    grid_sender,
    grid_owner,
    grid_node,
    mesh_latent,
    mesh_edge,
    halo_send,
    mesh_sender,
    mesh_receiver,
    enc_edge_in,
    enc_feat_proj,
    enc_edge_out,
    enc_edge_bias,
    enc_edge_gain,
    enc_node_in,
    enc_node_out,
    enc_node_bias,
    enc_node_gain,
    proc_edge_in,
    proc_edge_out,
    proc_edge_bias,
    proc_edge_gain,
    proc_node_in,
    proc_node_out,
    proc_node_bias,
    proc_node_gain,
):
    first = lax.all_gather(
        jnp.concatenate([enc_edge_in, enc_edge_out], 0), "lon", axis=1, tiled=True
    )
    inner = lax.all_gather(
        jnp.concatenate([enc_node_in, proc_edge_in, proc_edge_out, proc_node_in], 0),
        "lon",
        axis=1,
        tiled=True,
    )
    outer = lax.all_gather(
        jnp.concatenate([enc_node_out, proc_node_out], 1), "lon", axis=0, tiled=True
    )
    idx, fields = slots(
        grid_owner.reshape(1, -1), grid_sender.reshape(1, -1), grid_node.reshape(1, -1), grid_feat
    )
    proj = jnp.concatenate([enc_feat_proj, jnp.zeros((4, WIDTH), BF16)], 0)
    mesh_mid = gather_nodes(
        idx.reshape(PLANE, 2, 128),
        fields.reshape(PLANE, 8, 128),
        grid_latent,
        first[:WIDTH],
        proj,
        first[WIDTH:],
        enc_edge_bias,
        enc_edge_gain[None],
        mesh_latent,
        inner[:1024],
        outer[:, :WIDTH],
        enc_node_bias,
        enc_node_gain[None],
    )
    middle = lax.dynamic_slice_in_dim(mesh_mid, lax.axis_index("lon") * ROWS, ROWS, 0)
    halo = swap(mesh_mid[halo_send], "lat").reshape(NODES, WIDTH)
    edge_update, partial = edge_network(
        mesh_sender.reshape(1, -1),
        mesh_receiver.reshape(1, -1),
        mesh_edge,
        mesh_mid,
        halo,
        inner[1024:2560],
        inner[2560:3072],
        proc_edge_bias,
        proc_edge_gain[None],
    )
    parts = swap(partial.reshape(LON, ROWS, WIDTH), "lon")
    newest = node_network(
        middle, parts, inner[3072:], outer[:, WIDTH:], proc_node_bias, proc_node_gain[None]
    )
    tiles = jnp.moveaxis(newest.reshape(ROWS, LON, ROWS), 1, 0)
    mesh_update = swap(tiles, "lon").reshape(NODES, ROWS)
    return (mesh_update, edge_update)


def solution(mesh):
    placed = (
        P(("lat", "lon"), None),
        P(None, ("lat", "lon")),
        P(("lat", "lon")),
        P(("lat", "lon"), None),
        P(("lat", "lon")),
        P("lat", "lon"),
        P(("lat", "lon"), None),
        P("lat", None),
        P(("lat", "lon")),
        P(("lat", "lon")),
        P(None, "lon"),
        P(),
        P(None, "lon"),
        P(),
        P(),
        P(None, "lon"),
        P("lon", None),
        P(),
        P(),
        P(None, "lon"),
        P(None, "lon"),
        P(),
        P(),
        P(None, "lon"),
        P("lon", None),
        P(),
        P(),
    )
    return jax.shard_map(
        local,
        mesh=mesh,
        in_specs=placed,
        out_specs=(P("lat", "lon"), P(("lat", "lon"), None)),
        check_vma=False,
    )
```

```python
import jax
import jax.numpy as jnp
from jax import lax
from jax.experimental import pallas as pl
from jax.experimental.pallas import tpu as pltpu
from jax.sharding import PartitionSpec as P

F32 = jnp.float32
BF16 = jnp.bfloat16
LAT = 64
LON = 4
WIDTH = 512
NODES = 512
CAP = 64
ROWS = NODES // LON
PLANE = 32
DEPTH = 8
MESH = pl.DeviceIdType.MESH


def matmul(a, b):
    return jnp.dot(a, b, preferred_element_type=F32)


def matmul_t(a, b):
    return lax.dot_general(a, b, (((0,), (0,)), ((), ())), preferred_element_type=F32)


def matmul_nt(a, b):
    return lax.dot_general(a, b, (((1,), (1,)), ((), ())), preferred_element_type=F32)


def swish(t):
    return t / (1.0 + jnp.exp(-t))


def layer_norm(values, gain, offset):
    average = jnp.mean(values, axis=-1, keepdims=True)
    centred = values - average
    spread = jnp.mean(centred * centred, axis=-1, keepdims=True)
    return centred * lax.rsqrt(spread + 1e-05) * gain + offset


def one_hot(row, count):
    width = row.shape[1]
    return (lax.broadcasted_iota(jnp.int32, (count, width), 0) == row).astype(BF16)


def slots_kernel(owner, sender, node, feat, idx, fields):
    count = owner.shape[1]
    block = 128
    owners = owner[...]
    hit = one_hot(owners, LAT)
    row = lax.broadcasted_iota(jnp.int32, (block, block), 0)
    column = lax.broadcasted_iota(jnp.int32, (block, block), 1)
    above = (row < column).astype(BF16)
    carry = jnp.zeros((LAT, 1), F32)
    ranks = []
    for at in range(0, count, block):
        part = hit[:, at : at + block]
        wide = part.astype(F32)
        before = matmul(part, above) + carry
        ranks.append(jnp.sum(before * wide, axis=0, keepdims=True))
        carry = carry + jnp.sum(wide, axis=1, keepdims=True)
    rank = jnp.concatenate(ranks, axis=1).astype(jnp.int32)
    half = owners // 32
    target = (owners % 8) * 4 + (owners // 8) % 4
    at_target = one_hot(target, PLANE)
    place = one_hot(rank + half * CAP, 2 * CAP).astype(F32)
    named = node[...] + half * NODES + 1

    def put(values):
        return matmul_nt(at_target, (place * values.astype(F32)).astype(BF16))

    def put_whole(values):
        return (put(values // 32) * 32.0 + put(values % 32)).astype(jnp.int32)

    idx[:, :128] = put_whole(sender[...])
    idx[:, 128:] = put_whole(named) - 1
    for i in range(4):
        fields[:, i * 128 : (i + 1) * 128] = put(feat[i : i + 1, :])
    fields[:, 512:] = jnp.zeros((PLANE, 512), F32)


def slots(owner, sender, node, feat):
    return pl.pallas_call(
        slots_kernel,
        out_shape=[
            jax.ShapeDtypeStruct((PLANE, 256), jnp.int32),
            jax.ShapeDtypeStruct((PLANE, 1024), F32),
        ],
        name="slots",
    )(owner, sender, node, feat)


def remote(source, target, send, receive, where):
    return pltpu.make_async_remote_copy(
        src_ref=source,
        dst_ref=target,
        send_sem=send,
        recv_sem=receive,
        device_id=where,
        device_id_type=MESH,
    )


COLUMNS = (True, True, True, False, True, True, True, False)


def layer_kernel(
    idx, feat, grid, mesh, halo_rows, edges, sender, receiver, proj,
    edge_bias, edge_gain, node_bias, node_gain, proc_bias, proc_gain, last_bias, last_gain,
    k0, k1, k2, k3, k4, k5, k6, k7,
    out, edge_out,
    w0, w1, w2, w3, w4, w5, w6, w7,
    send, got, got_ids, acc, part, plane, share, aggregate, base, middle, whole,
    outgoing, halo, pre_all, incoming, newest, update,
    s_msg, r_msg, s_ids, r_ids, s_z, r_z, s_share, r_share, s_base, r_base, s_mid, r_mid,
    s_halo, r_halo, s_inc, r_inc, s_new, r_new,
    s_part, r_part, s_cross, r_cross, s_fwd, r_fwd,
):
    pieces = (k0, k1, k2, k3, k4, k5, k6, k7)
    weights = (w0, w1, w2, w3, w4, w5, w6, w7)
    lat = lax.axis_index("lat")
    lon = lax.axis_index("lon")
    z = lat // 8
    cell = lat % 8
    place = cell * LON + lon
    owner = z % 4 == lon

    def at_place(t):
        return {"lat": z * 8 + t // LON, "lon": t % LON}

    def at_depth(depth):
        return {"lat": depth * 8 + cell, "lon": lon}

    def at_lon(other):
        return {"lat": lat, "lon": other}

    def beside(step):
        return at_lon((lon + step) % LON)

    def behind(step):
        return (lon - step + LON) % LON

    def rows_of(q):
        return pl.ds(pl.multiple_of(q * ROWS, ROWS), ROWS)

    mine = rows_of(lon)
    barrier = pltpu.get_barrier_semaphore()

    def greet(d, _):
        pl.semaphore_signal(
            barrier, inc=1, device_id={"lat": (lat + d) % LAT, "lon": lon}, device_id_type=MESH
        )
        return 0

    lax.fori_loop(1, LAT, greet, 0)
    for step in range(1, LON):

        def greet_plane(c, _):
            pl.semaphore_signal(
                barrier,
                inc=1,
                device_id={"lat": z * 8 + (cell + c) % 8, "lon": (lon + step) % LON},
                device_id_type=MESH,
            )
            return 0

        lax.fori_loop(0, 8, greet_plane, 0)

    def target(d):
        return (place + d) % PLANE

    def pick(s, _):
        one, two = target(2 * s), target(2 * s + 1)
        names = jnp.concatenate([idx[one][0:1, :], idx[two][0:1, :]], axis=1)
        rows = matmul_t(one_hot(names, WIDTH), grid[...]).astype(BF16)
        send[2 * s] = rows[:128]
        send[2 * s + 1] = rows[128:]
        return 0

    def compute(d):
        one, two = target(d), target(d + 1)
        features = jnp.concatenate([feat[one], feat[two]], axis=1).astype(BF16)
        rows = jnp.concatenate([send[d], send[d + 1]], axis=0)
        pre = matmul(rows, w0[...]) + (matmul_t(features, proj[...]) + edge_bias[0:1, :])
        raw = matmul_nt(swish(pre).astype(BF16), w1[...])
        message = layer_norm(raw, edge_gain[...], edge_bias[1:2, :]).astype(BF16)
        send[d] = message[:128]
        send[d + 1] = message[128:]

    def message_copy(d):
        return remote(send.at[d], got.at[d], s_msg.at[d], r_msg.at[d], at_place(target(d)))

    def ids_copy(d):
        return remote(idx.at[target(d)], got_ids.at[d], s_ids.at[d], r_ids.at[d], at_place(target(d)))

    def base_copy(step, writer):
        return remote(
            mesh.at[rows_of((lon + step) % LON), :],
            base.at[:, rows_of(writer)],
            s_base.at[step],
            r_base.at[step],
            beside(step),
        )

    partner = lon + 1 - 2 * (lon % 2)
    cross = (lon + 2) % LON
    corner = partner + 2 - 4 * (partner // 2)

    def block(i, q):
        return weights[i].at[:, rows_of(q)] if COLUMNS[i] else weights[i].at[rows_of(q), :]

    def to_partner(i, q):
        return remote(pieces[i], block(i, q), s_part.at[i], r_part.at[i], at_lon(partner))

    def to_cross(i, q):
        return remote(pieces[i], block(i, q), s_cross.at[i], r_cross.at[i], at_lon(cross))

    def forward(i, q):
        return remote(block(i, q), block(i, q), s_fwd.at[i], r_fwd.at[i], at_lon(partner))

    def offer(i):
        to_cross(i, lon).start()
        to_partner(i, lon).start()

    def relay(i):
        to_cross(i, cross).wait_recv()
        forward(i, cross).start()

    def settle(i):
        to_partner(i, partner).wait_recv()
        forward(i, corner).wait_recv()

    lax.fori_loop(0, 4, pick, 0)
    pl.semaphore_wait(barrier, LAT - 1 + 24)
    offer(0)
    offer(1)

    def start_ids(d, _):
        ids_copy(d).start()
        return 0

    lax.fori_loop(1, PLANE, start_ids, 0)
    for step in range(1, LON):
        base_copy(step, lon).start()
    for i in range(8):
        if COLUMNS[i]:
            weights[i][:, mine] = pieces[i][...]
        else:
            weights[i][mine, :] = pieces[i][...]
    base[:, mine] = mesh[mine, :]
    lax.fori_loop(4, PLANE // 2, pick, 0)
    relay(0)
    relay(1)
    settle(0)
    settle(1)

    compute(0)
    got[0] = send[0]
    got_ids[0] = idx[place]
    message_copy(1).start()

    def start_messages(s, _):
        compute(2 * s)
        message_copy(2 * s).start()
        message_copy(2 * s + 1).start()
        return 0

    lax.fori_loop(1, PLANE // 2, start_messages, 0)
    for i in range(2, 8):
        offer(i)

    acc[...] = jnp.zeros_like(acc)

    def take(g):
        ids = jnp.concatenate([got_ids[4 * g + i][1:2, :] for i in range(4)], axis=1)
        rows = jnp.concatenate([got[4 * g + i] for i in range(4)], axis=0)
        acc[...] += matmul(one_hot(ids, 2 * NODES), rows)

    def arrive(d):
        ids_copy(d).wait_recv()
        message_copy(d).wait_recv()

    for d in range(1, 4):
        arrive(d)
    take(0)

    def collect(g, _):
        for i in range(4):
            arrive(4 * g + i)
        take(g)
        return 0

    lax.fori_loop(1, PLANE // 4, collect, 0)

    def depth_copy(j, q):
        depth = lon + 4 * j
        away = (depth - z + DEPTH) % DEPTH
        return remote(
            part.at[pl.ds(j * NODES + q * ROWS, ROWS), :],
            plane.at[away, pl.ds(q * ROWS, ROWS), :],
            s_z.at[j, q],
            r_z.at[away, q],
            at_depth(depth),
        )

    for q in range(LON):
        for j in range(2):
            rows = pl.ds(j * NODES + q * ROWS, ROWS)
            part[rows, :] = acc[rows, :].astype(BF16)

            @pl.when(z != lon + 4 * j)
            def _():
                depth_copy(j, q).start()

    relay(2)
    relay(3)

    def share_copy(q):
        return remote(share.at[q], aggregate, s_share.at[q], r_share.at[0], at_lon(q))

    @pl.when(owner)
    def _():
        for q in range(LON):
            first = pl.multiple_of((z // 4) * NODES + q * ROWS, ROWS)
            total = acc[pl.ds(first, ROWS), :]
            for away in range(1, DEPTH):
                remote(
                    part.at[pl.ds(0, ROWS), :],
                    plane.at[away, pl.ds(q * ROWS, ROWS), :],
                    s_z.at[0, q],
                    r_z.at[away, q],
                    at_depth(z),
                ).wait_recv()
                total = total + plane[away, pl.ds(q * ROWS, ROWS), :].astype(F32)
            rounded = total.astype(BF16)

            @pl.when(lon == q)
            def _():
                aggregate[...] = rounded

            @pl.when(lon != q)
            def _():
                share[q] = rounded
                share_copy(q).start()

    settle(2)
    settle(3)
    for step in range(1, LON):
        base_copy(step, behind(step)).wait_recv()

    def node_network(before, pre_base, summed, w_in, w_out, bias, gain):
        pre = pre_base + matmul(summed, w_in[WIDTH:, :]) + bias[0:1, :]
        raw = matmul(swish(pre).astype(BF16), w_out[...])
        return (before.astype(F32) + layer_norm(raw, gain[...], bias[1:2, :])).astype(BF16)

    pre_base = matmul(base[...], w2[:WIDTH, :])

    @pl.when(z % 4 != lon)
    def _():
        share_copy(0).wait_recv()

    middle[...] = node_network(base[...], pre_base, aggregate[...], w2, w3, node_bias, node_gain)

    def middle_copy(step, writer):
        return remote(middle, whole.at[rows_of(writer), :], s_mid.at[step], r_mid.at[step], beside(step))

    for step in range(1, LON):
        middle_copy(step, lon).start()
    whole[mine, :] = middle[...]
    for i in range(4, 8):
        relay(i)
    for step in range(1, LON):
        middle_copy(step, behind(step)).wait_recv()

    chosen = matmul_t(one_hot(halo_rows[...], NODES), whole[...])
    outgoing[...] = chosen.reshape(LAT, 8, WIDTH).astype(BF16)

    def halo_copy(d, writer):
        other = (lat + d) % LAT
        return remote(
            outgoing.at[other], halo.at[writer], s_halo.at[d], r_halo.at[d], {"lat": other, "lon": lon}
        )

    def start_halo(d, _):
        halo_copy(d, lat).start()
        return 0

    lax.fori_loop(1, LAT, start_halo, 0)
    halo[lat] = outgoing[lat]
    for i in range(4, 8):
        settle(i)

    def begin(c, _):
        rows = pl.ds(pl.multiple_of(c * 256, 256), 256)
        sent = matmul_t(one_hot(sender[c], NODES), whole[...]).astype(BF16)
        received = matmul_t(one_hot(receiver[c], NODES), whole[...]).astype(BF16)
        pre = matmul(edges[rows, :], w4[:WIDTH, :])
        pre = pre + matmul(sent, w4[WIDTH : 2 * WIDTH, :])
        pre = pre + matmul(received, w4[2 * WIDTH :, :])
        pre_all[rows, :] = pre + proc_bias[0:1, :]
        return 0

    lax.fori_loop(0, 4, begin, 0)
    last_base = matmul(middle[...], w6[:WIDTH, :])

    def end_halo(d, _):
        halo_copy(d, (lat - d + LAT) % LAT).wait_recv()
        return 0

    lax.fori_loop(1, LAT, end_halo, 0)
    incoming[...] = jnp.zeros_like(incoming)
    table = halo[...].astype(F32).reshape(NODES, WIDTH).astype(BF16)

    def finish(c, _):
        rows = pl.ds(pl.multiple_of(c * 256, 256), 256)
        sent = matmul_t(one_hot(sender[c] - NODES, NODES), table).astype(BF16)
        pre = pre_all[rows, :] + matmul(sent, w4[WIDTH : 2 * WIDTH, :])
        raw = matmul_nt(swish(pre).astype(BF16), w5[...])
        old = edges[rows, :].astype(F32)
        updated = (old + layer_norm(raw, proc_gain[...], proc_bias[1:2, :])).astype(BF16)
        edge_out[rows, :] = updated
        incoming[...] += matmul(one_hot(receiver[c], NODES), updated)
        return 0

    lax.fori_loop(0, 4, finish, 0)
    for q in range(LON):
        for j in range(2):

            @pl.when(z != lon + 4 * j)
            def _():
                depth_copy(j, q).wait_send()

    for q in range(LON):
        share_rows = pl.ds(q * ROWS, ROWS)
        part[share_rows, :] = incoming[share_rows, :].astype(BF16)

    def incoming_copy(step):
        return remote(
            part.at[rows_of((lon + step) % LON), :],
            plane.at[0, pl.ds(step * ROWS, ROWS), :],
            s_inc.at[step],
            r_inc.at[step],
            beside(step),
        )

    for step in range(1, LON):
        incoming_copy(step).start()
    total = incoming[mine, :]
    for step in range(1, LON):
        incoming_copy(step).wait_recv()
        total = total + plane[0, step * ROWS : (step + 1) * ROWS, :].astype(F32)
    newest[...] = node_network(middle[...], last_base, total.astype(BF16), w6, w7, last_bias, last_gain)

    def newest_copy(step, writer):
        return remote(
            newest.at[:, rows_of((lon + step) % LON)],
            update.at[rows_of(writer), :],
            s_new.at[step],
            r_new.at[step],
            beside(step),
        )

    for step in range(1, LON):
        newest_copy(step, lon).start()
    update[mine, :] = newest[:, mine]

    def sent(d, _):
        ids_copy(d).wait_send()
        message_copy(d).wait_send()
        return 0

    lax.fori_loop(1, PLANE, sent, 0)

    def sent_halo(d, _):
        halo_copy(d, lat).wait_send()
        return 0

    lax.fori_loop(1, LAT, sent_halo, 0)
    for i in range(8):
        to_cross(i, lon).wait_send()
        to_partner(i, lon).wait_send()
        forward(i, cross).wait_send()
    for step in range(1, LON):
        base_copy(step, lon).wait_send()
        middle_copy(step, lon).wait_send()
        incoming_copy(step).wait_send()
        newest_copy(step, lon).wait_send()

    @pl.when(owner)
    def _():
        for q in range(LON):

            @pl.when(lon != q)
            def _():
                share_copy(q).wait_send()

    for step in range(1, LON):
        newest_copy(step, behind(step)).wait_recv()
    out[...] = update[...]


def layer(*operands):
    dma = pltpu.SemaphoreType.DMA
    shapes = [
        (WIDTH, WIDTH), (WIDTH, WIDTH), (2 * WIDTH, WIDTH), (WIDTH, WIDTH),
        (3 * WIDTH, WIDTH), (WIDTH, WIDTH), (2 * WIDTH, WIDTH), (WIDTH, WIDTH),
        (PLANE, 128, WIDTH), (PLANE, 128, WIDTH),
    ]
    return pl.pallas_call(
        layer_kernel,
        in_specs=[pl.BlockSpec(memory_space=pltpu.VMEM)] * len(operands),
        out_specs=[pl.BlockSpec(memory_space=pltpu.VMEM)] * 2,
        out_shape=[
            jax.ShapeDtypeStruct((NODES, ROWS), BF16),
            jax.ShapeDtypeStruct((1024, WIDTH), BF16),
        ],
        scratch_shapes=[pltpu.VMEM(shape, BF16) for shape in shapes]
        + [
            pltpu.VMEM((PLANE, 2, 128), jnp.int32),
            pltpu.VMEM((2 * NODES, WIDTH), F32),
            pltpu.VMEM((2 * NODES, WIDTH), BF16),
            pltpu.VMEM((DEPTH, NODES, WIDTH), BF16),
            pltpu.VMEM((LON, ROWS, WIDTH), BF16),
            pltpu.VMEM((ROWS, WIDTH), BF16),
            pltpu.VMEM((ROWS, WIDTH), BF16),
            pltpu.VMEM((ROWS, WIDTH), BF16),
            pltpu.VMEM((NODES, WIDTH), BF16),
            pltpu.VMEM((LAT, 8, WIDTH), BF16),
            pltpu.VMEM((LAT, 8, WIDTH), BF16),
            pltpu.VMEM((1024, WIDTH), F32),
            pltpu.VMEM((NODES, WIDTH), F32),
            pltpu.VMEM((ROWS, WIDTH), BF16),
            pltpu.VMEM((NODES, ROWS), BF16),
            dma((PLANE,)), dma((PLANE,)), dma((PLANE,)), dma((PLANE,)),
            dma((2, LON)), dma((DEPTH, LON)), dma((LON,)), dma((1,)),
            dma((LON,)), dma((LON,)), dma((LON,)), dma((LON,)),
            dma((LAT,)), dma((LAT,)), dma((LON,)), dma((LON,)), dma((LON,)), dma((LON,)),
            dma((8,)), dma((8,)), dma((8,)), dma((8,)), dma((8,)), dma((8,)),
        ],
        compiler_params=pltpu.CompilerParams(
            collective_id=0, has_side_effects=True, vmem_limit_bytes=60 * 1024 * 1024
        ),
        name="layer",
    )(*operands)


def local(
    grid_latent,
    grid_feat,
    grid_sender,
    grid_owner,
    grid_node,
    mesh_latent,
    mesh_edge,
    halo_send,
    mesh_sender,
    mesh_receiver,
    enc_edge_in,
    enc_feat_proj,
    enc_edge_out,
    enc_edge_bias,
    enc_edge_gain,
    enc_node_in,
    enc_node_out,
    enc_node_bias,
    enc_node_gain,
    proc_edge_in,
    proc_edge_out,
    proc_edge_bias,
    proc_edge_gain,
    proc_node_in,
    proc_node_out,
    proc_node_bias,
    proc_node_gain,
):
    idx, fields = slots(
        grid_owner.reshape(1, -1), grid_sender.reshape(1, -1), grid_node.reshape(1, -1), grid_feat
    )
    proj = jnp.concatenate([enc_feat_proj, jnp.zeros((4, WIDTH), BF16)], 0)
    return layer(
        idx.reshape(PLANE, 2, 128),
        fields.reshape(PLANE, 8, 128),
        grid_latent,
        mesh_latent,
        halo_send.reshape(1, -1),
        mesh_edge,
        mesh_sender.reshape(4, 1, 256),
        mesh_receiver.reshape(4, 1, 256),
        proj,
        enc_edge_bias,
        enc_edge_gain[None],
        enc_node_bias,
        enc_node_gain[None],
        proc_edge_bias,
        proc_edge_gain[None],
        proc_node_bias,
        proc_node_gain[None],
        enc_edge_in,
        enc_edge_out,
        enc_node_in,
        enc_node_out,
        proc_edge_in,
        proc_edge_out,
        proc_node_in,
        proc_node_out,
    )


def solution(mesh):
    placed = (
        P(("lat", "lon"), None),
        P(None, ("lat", "lon")),
        P(("lat", "lon")),
        P(("lat", "lon"), None),
        P(("lat", "lon")),
        P("lat", "lon"),
        P(("lat", "lon"), None),
        P("lat", None),
        P(("lat", "lon")),
        P(("lat", "lon")),
        P(None, "lon"),
        P(),
        P(None, "lon"),
        P(),
        P(),
        P(None, "lon"),
        P("lon", None),
        P(),
        P(),
        P(None, "lon"),
        P(None, "lon"),
        P(),
        P(),
        P(None, "lon"),
        P("lon", None),
        P(),
        P(),
    )
    return jax.shard_map(
        local,
        mesh=mesh,
        in_specs=placed,
        out_specs=(P("lat", "lon"), P(("lat", "lon"), None)),
        check_vma=False,
    )
```

```python
import jax
import jax.numpy as jnp
from jax import lax
from jax.experimental import pallas as pl
from jax.experimental.pallas import tpu as pltpu
from jax.sharding import PartitionSpec as P

F32 = jnp.float32
BF16 = jnp.bfloat16
LAT = 64
LON = 4
WIDTH = 512
NODES = 512
CAP = 64
ROWS = NODES // LON
PLANE = 32
DEPTH = 8
HALF = WIDTH // 2
MESH = pl.DeviceIdType.MESH


def matmul(a, b):
    return jnp.dot(a, b, preferred_element_type=F32)


def matmul_t(a, b):
    return lax.dot_general(a, b, (((0,), (0,)), ((), ())), preferred_element_type=F32)


def matmul_nt(a, b):
    return lax.dot_general(a, b, (((1,), (1,)), ((), ())), preferred_element_type=F32)


def swish(t):
    return t / (1.0 + jnp.exp(-t))


def layer_norm(values, gain, offset):
    average = jnp.mean(values, axis=-1, keepdims=True)
    centred = values - average
    spread = jnp.mean(centred * centred, axis=-1, keepdims=True)
    return centred * lax.rsqrt(spread + 1e-05) * gain + offset


def one_hot(row, count):
    width = row.shape[1]
    return (lax.broadcasted_iota(jnp.int32, (count, width), 0) == row).astype(BF16)


def slots_kernel(owner, sender, node, feat, idx, fields):
    count = owner.shape[1]
    block = 128
    owners = owner[...]
    hit = one_hot(owners, LAT)
    row = lax.broadcasted_iota(jnp.int32, (block, block), 0)
    column = lax.broadcasted_iota(jnp.int32, (block, block), 1)
    above = (row < column).astype(BF16)
    carry = jnp.zeros((LAT, 1), F32)
    ranks = []
    for at in range(0, count, block):
        part = hit[:, at : at + block]
        wide = part.astype(F32)
        before = matmul(part, above) + carry
        ranks.append(jnp.sum(before * wide, axis=0, keepdims=True))
        carry = carry + jnp.sum(wide, axis=1, keepdims=True)
    rank = jnp.concatenate(ranks, axis=1).astype(jnp.int32)
    half = owners // 32
    target = (owners % 8) * 4 + (owners // 8) % 2 * 2 + (owners // 16) % 2
    at_target = one_hot(target, PLANE)
    place = one_hot(rank + half * CAP, 2 * CAP).astype(F32)
    named = node[...] + half * NODES + 1

    def put(values):
        return matmul_nt(at_target, (place * values.astype(F32)).astype(BF16))

    def put_whole(values):
        return (put(values // 32) * 32.0 + put(values % 32)).astype(jnp.int32)

    idx[:, :128] = put_whole(sender[...])
    idx[:, 128:] = put_whole(named) - 1
    for i in range(4):
        fields[:, i * 128 : (i + 1) * 128] = put(feat[i : i + 1, :])
    fields[:, 512:] = jnp.zeros((PLANE, 512), F32)


def slots(owner, sender, node, feat):
    return pl.pallas_call(
        slots_kernel,
        out_shape=[
            jax.ShapeDtypeStruct((PLANE, 256), jnp.int32),
            jax.ShapeDtypeStruct((PLANE, 1024), F32),
        ],
        name="slots",
    )(owner, sender, node, feat)


def remote(source, target, send, receive, where):
    return pltpu.make_async_remote_copy(
        src_ref=source,
        dst_ref=target,
        send_sem=send,
        recv_sem=receive,
        device_id=where,
        device_id_type=MESH,
    )


COLUMNS = (True, True, True, False, True, True, True, False)


def layer_kernel(
    idx, feat, grid, mesh, halo_rows, edges, sender, receiver, proj,
    edge_bias, edge_gain, node_bias, node_gain, proc_bias, proc_gain, last_bias, last_gain,
    k0, k1, k2, k3, k4, k5, k6, k7,
    out, edge_out,
    w0, w1, w2, w3, w4, w5, w6, w7,
    send, got, got_ids, acc, part, plane, share, aggregate, base, middle, whole,
    outgoing, halo, pre_all, incoming, newest, update,
    s_msg, r_msg, s_ids, r_ids, s_z, r_z, s_share, r_share, s_base, r_base, s_mid, r_mid,
    s_halo, r_halo, s_inc, r_inc, s_new, r_new,
    s_part, r_part, s_cross, r_cross, s_fwd, r_fwd,
):
    pieces = (k0, k1, k2, k3, k4, k5, k6, k7)
    weights = (w0, w1, w2, w3, w4, w5, w6, w7)
    lat = lax.axis_index("lat")
    lon = lax.axis_index("lon")
    z = lat // 8
    cell = lat % 8
    place = cell * LON + lon
    shelf = 2 * (lon % 2) + lon // 2
    owner = z % 4 == shelf

    def at_place(t):
        return {"lat": z * 8 + t // LON, "lon": t % LON}

    def at_depth(depth):
        return {"lat": depth * 8 + cell, "lon": lon}

    def at_lon(other):
        return {"lat": lat, "lon": other}

    def beside(step):
        return at_lon((lon + step) % LON)

    def behind(step):
        return (lon - step + LON) % LON

    def rows_of(q):
        return pl.ds(pl.multiple_of(q * ROWS, ROWS), ROWS)

    mine = rows_of(lon)
    barrier = pltpu.get_barrier_semaphore()

    def greet(d, _):
        pl.semaphore_signal(
            barrier, inc=1, device_id={"lat": (lat + d) % LAT, "lon": lon}, device_id_type=MESH
        )
        return 0

    lax.fori_loop(1, LAT, greet, 0)
    for step in range(1, LON):

        def greet_plane(c, _):
            pl.semaphore_signal(
                barrier,
                inc=1,
                device_id={"lat": z * 8 + (cell + c) % 8, "lon": (lon + step) % LON},
                device_id_type=MESH,
            )
            return 0

        lax.fori_loop(0, 8, greet_plane, 0)

    def target(d):
        turn = (d * 13) % PLANE
        row = (place // 8 + turn // 8) % 4
        column = (place // 2 + turn // 2) % 4
        return row * 8 + column * 2 + (place + turn) % 2

    def pick(s, _):
        one, two = target(2 * s), target(2 * s + 1)
        names = jnp.concatenate([idx[one][0:1, :], idx[two][0:1, :]], axis=1)
        rows = matmul_t(one_hot(names, WIDTH), grid[...]).astype(BF16)
        send[2 * s] = rows[:128]
        send[2 * s + 1] = rows[128:]
        return 0

    def compute(d):
        one, two = target(d), target(d + 1)
        features = jnp.concatenate([feat[one], feat[two]], axis=1).astype(BF16)
        rows = jnp.concatenate([send[d], send[d + 1]], axis=0)
        pre = matmul(rows, w0[...]) + (matmul_t(features, proj[...]) + edge_bias[0:1, :])
        raw = matmul_nt(swish(pre).astype(BF16), w1[...])
        message = layer_norm(raw, edge_gain[...], edge_bias[1:2, :]).astype(BF16)
        send[d] = message[:128]
        send[d + 1] = message[128:]

    def message_copy(d, half):
        columns = pl.ds(half * HALF, HALF)
        return remote(
            send.at[d, :, columns],
            got.at[d, :, columns],
            s_msg.at[half, d],
            r_msg.at[half, d],
            at_place(target(d)),
        )

    def ids_copy(d):
        return remote(idx.at[target(d)], got_ids.at[d], s_ids.at[d], r_ids.at[d], at_place(target(d)))

    def base_copy(step, writer):
        return remote(
            mesh.at[rows_of((lon + step) % LON), :],
            base.at[:, rows_of(writer)],
            s_base.at[step],
            r_base.at[step],
            beside(step),
        )

    partner = lon + 1 - 2 * (lon % 2)
    cross = (lon + 2) % LON
    corner = partner + 2 - 4 * (partner // 2)

    def block(i, q):
        return weights[i].at[:, rows_of(q)] if COLUMNS[i] else weights[i].at[rows_of(q), :]

    def to_partner(i, q):
        return remote(pieces[i], block(i, q), s_part.at[i], r_part.at[i], at_lon(partner))

    def to_cross(i, q):
        return remote(pieces[i], block(i, q), s_cross.at[i], r_cross.at[i], at_lon(cross))

    def forward(i, q):
        return remote(block(i, q), block(i, q), s_fwd.at[i], r_fwd.at[i], at_lon(partner))

    def offer(i):
        to_cross(i, lon).start()
        to_partner(i, lon).start()

    def relay(i):
        to_cross(i, cross).wait_recv()
        forward(i, cross).start()

    def settle(i):
        to_partner(i, partner).wait_recv()
        forward(i, corner).wait_recv()

    lax.fori_loop(0, 4, pick, 0)
    pl.semaphore_wait(barrier, LAT - 1 + 24)
    offer(0)
    offer(1)

    def start_ids(d, _):
        ids_copy(d).start()
        return 0

    lax.fori_loop(1, PLANE, start_ids, 0)
    for step in range(1, LON):
        base_copy(step, lon).start()
    for i in range(8):
        if COLUMNS[i]:
            weights[i][:, mine] = pieces[i][...]
        else:
            weights[i][mine, :] = pieces[i][...]
    base[:, mine] = mesh[mine, :]
    lax.fori_loop(4, PLANE // 2, pick, 0)
    relay(0)
    relay(1)
    settle(0)
    settle(1)

    compute(0)
    got[0] = send[0]
    got_ids[0] = idx[place]
    message_copy(1, 0).start()

    def start_messages(s, _):
        compute(2 * s)
        message_copy(2 * s, 0).start()
        message_copy(2 * s + 1, 0).start()
        return 0

    lax.fori_loop(1, PLANE // 2, start_messages, 0)

    def start_rest(d, _):
        message_copy(d, 1).start()
        return 0

    lax.fori_loop(1, PLANE, start_rest, 0)
    for i in range(2, 8):
        offer(i)

    acc[...] = jnp.zeros_like(acc)

    def take(g, half):
        columns = slice(half * HALF, (half + 1) * HALF)
        ids = jnp.concatenate([got_ids[4 * g + i][1:2, :] for i in range(4)], axis=1)
        rows = jnp.concatenate([got[4 * g + i, :, columns] for i in range(4)], axis=0)
        acc[:, columns] += matmul(one_hot(ids, 2 * NODES), rows)

    def arrive(d, half):
        if half == 0:
            ids_copy(d).wait_recv()
        message_copy(d, half).wait_recv()

    def collect(half):
        for d in range(1, 4):
            arrive(d, half)
        take(0, half)

        def group(g, _):
            for i in range(4):
                arrive(4 * g + i, half)
            take(g, half)
            return 0

        lax.fori_loop(1, PLANE // 4, group, 0)

    def depth_copy(j, q):
        depth = shelf + 4 * j
        away = (depth - z + DEPTH) % DEPTH
        if q == LON:
            source = part.at[pl.ds(j * NODES, NODES), pl.ds(0, HALF)]
            goal = plane.at[away, :, pl.ds(0, HALF)]
        else:
            source = part.at[pl.ds(j * NODES + q * ROWS, ROWS), pl.ds(HALF, HALF)]
            goal = plane.at[away, pl.ds(q * ROWS, ROWS), pl.ds(HALF, HALF)]
        return remote(source, goal, s_z.at[j, q], r_z.at[away, q], at_depth(depth))

    collect(0)
    part[:, :HALF] = acc[:, :HALF].astype(BF16)
    for j in range(2):

        @pl.when(z != shelf + 4 * j)
        def _():
            depth_copy(j, LON).start()

    collect(1)
    for q in range(LON):
        for j in range(2):
            rows = pl.ds(j * NODES + q * ROWS, ROWS)
            part[rows, HALF:] = acc[rows, HALF:].astype(BF16)

            @pl.when(z != shelf + 4 * j)
            def _():
                depth_copy(j, q).start()

    relay(2)
    relay(3)

    def share_copy(q):
        return remote(share.at[q], aggregate, s_share.at[q], r_share.at[0], at_lon(q))

    def depth_arrival(away, q):
        if q == LON:
            source = part.at[pl.ds(0, NODES), pl.ds(0, HALF)]
            goal = plane.at[away, :, pl.ds(0, HALF)]
        else:
            source = part.at[pl.ds(0, ROWS), pl.ds(HALF, HALF)]
            goal = plane.at[away, pl.ds(q * ROWS, ROWS), pl.ds(HALF, HALF)]
        return remote(source, goal, s_z.at[0, q], r_z.at[away, q], at_depth(z))

    @pl.when(owner)
    def _():
        for away in range(1, DEPTH):
            depth_arrival(away, LON).wait_recv()
        for q in range(LON):
            first = pl.multiple_of((z // 4) * NODES + q * ROWS, ROWS)
            total = acc[pl.ds(first, ROWS), :]
            for away in range(1, DEPTH):
                depth_arrival(away, q).wait_recv()
                total = total + plane[away, pl.ds(q * ROWS, ROWS), :].astype(F32)
            rounded = total.astype(BF16)

            @pl.when(lon == q)
            def _():
                aggregate[...] = rounded

            @pl.when(lon != q)
            def _():
                share[q] = rounded
                share_copy(q).start()

    settle(2)
    settle(3)
    for step in range(1, LON):
        base_copy(step, behind(step)).wait_recv()

    def node_network(before, pre_base, summed, w_in, w_out, bias, gain):
        pre = pre_base + matmul(summed, w_in[WIDTH:, :]) + bias[0:1, :]
        raw = matmul(swish(pre).astype(BF16), w_out[...])
        return (before.astype(F32) + layer_norm(raw, gain[...], bias[1:2, :])).astype(BF16)

    pre_base = matmul(base[...], w2[:WIDTH, :])

    @pl.when(z % 4 != shelf)
    def _():
        share_copy(0).wait_recv()

    middle[...] = node_network(base[...], pre_base, aggregate[...], w2, w3, node_bias, node_gain)

    def middle_copy(step, writer):
        return remote(middle, whole.at[rows_of(writer), :], s_mid.at[step], r_mid.at[step], beside(step))

    for step in range(1, LON):
        middle_copy(step, lon).start()
    whole[mine, :] = middle[...]
    for i in range(4, 8):
        relay(i)
    for step in range(1, LON):
        middle_copy(step, behind(step)).wait_recv()

    chosen = matmul_t(one_hot(halo_rows[...], NODES), whole[...])
    outgoing[...] = chosen.reshape(LAT, 8, WIDTH).astype(BF16)

    def halo_copy(d, writer):
        other = (lat + d) % LAT
        return remote(
            outgoing.at[other], halo.at[writer], s_halo.at[d], r_halo.at[d], {"lat": other, "lon": lon}
        )

    def start_halo(d, _):
        halo_copy(d, lat).start()
        return 0

    lax.fori_loop(1, LAT, start_halo, 0)
    halo[lat] = outgoing[lat]
    for i in range(4, 8):
        settle(i)

    def begin(c, _):
        rows = pl.ds(pl.multiple_of(c * 256, 256), 256)
        sent = matmul_t(one_hot(sender[c], NODES), whole[...]).astype(BF16)
        received = matmul_t(one_hot(receiver[c], NODES), whole[...]).astype(BF16)
        pre = matmul(edges[rows, :], w4[:WIDTH, :])
        pre = pre + matmul(sent, w4[WIDTH : 2 * WIDTH, :])
        pre = pre + matmul(received, w4[2 * WIDTH :, :])
        pre_all[rows, :] = pre + proc_bias[0:1, :]
        return 0

    lax.fori_loop(0, 4, begin, 0)
    last_base = matmul(middle[...], w6[:WIDTH, :])

    def end_halo(d, _):
        halo_copy(d, (lat - d + LAT) % LAT).wait_recv()
        return 0

    lax.fori_loop(1, LAT, end_halo, 0)
    incoming[...] = jnp.zeros_like(incoming)
    table = halo[...].astype(F32).reshape(NODES, WIDTH).astype(BF16)

    def finish(c, _):
        rows = pl.ds(pl.multiple_of(c * 256, 256), 256)
        sent = matmul_t(one_hot(sender[c] - NODES, NODES), table).astype(BF16)
        pre = pre_all[rows, :] + matmul(sent, w4[WIDTH : 2 * WIDTH, :])
        raw = matmul_nt(swish(pre).astype(BF16), w5[...])
        old = edges[rows, :].astype(F32)
        updated = (old + layer_norm(raw, proc_gain[...], proc_bias[1:2, :])).astype(BF16)
        edge_out[rows, :] = updated
        incoming[...] += matmul(one_hot(receiver[c], NODES), updated)
        return 0

    lax.fori_loop(0, 4, finish, 0)
    for q in range(LON + 1):
        for j in range(2):

            @pl.when(z != shelf + 4 * j)
            def _():
                depth_copy(j, q).wait_send()

    for q in range(LON):
        share_rows = pl.ds(q * ROWS, ROWS)
        part[share_rows, :] = incoming[share_rows, :].astype(BF16)

    def incoming_copy(step):
        return remote(
            part.at[rows_of((lon + step) % LON), :],
            plane.at[0, pl.ds(step * ROWS, ROWS), :],
            s_inc.at[step],
            r_inc.at[step],
            beside(step),
        )

    for step in range(1, LON):
        incoming_copy(step).start()
    total = incoming[mine, :]
    for step in range(1, LON):
        incoming_copy(step).wait_recv()
        total = total + plane[0, step * ROWS : (step + 1) * ROWS, :].astype(F32)
    newest[...] = node_network(middle[...], last_base, total.astype(BF16), w6, w7, last_bias, last_gain)

    def newest_copy(step, writer):
        return remote(
            newest.at[:, rows_of((lon + step) % LON)],
            update.at[rows_of(writer), :],
            s_new.at[step],
            r_new.at[step],
            beside(step),
        )

    for step in range(1, LON):
        newest_copy(step, lon).start()
    update[mine, :] = newest[:, mine]

    def sent(d, _):
        ids_copy(d).wait_send()
        message_copy(d, 0).wait_send()
        message_copy(d, 1).wait_send()
        return 0

    lax.fori_loop(1, PLANE, sent, 0)

    def sent_halo(d, _):
        halo_copy(d, lat).wait_send()
        return 0

    lax.fori_loop(1, LAT, sent_halo, 0)
    for i in range(8):
        to_cross(i, lon).wait_send()
        to_partner(i, lon).wait_send()
        forward(i, cross).wait_send()
    for step in range(1, LON):
        base_copy(step, lon).wait_send()
        middle_copy(step, lon).wait_send()
        incoming_copy(step).wait_send()
        newest_copy(step, lon).wait_send()

    @pl.when(owner)
    def _():
        for q in range(LON):

            @pl.when(lon != q)
            def _():
                share_copy(q).wait_send()

    for step in range(1, LON):
        newest_copy(step, behind(step)).wait_recv()
    out[...] = update[...]


def layer(*operands):
    dma = pltpu.SemaphoreType.DMA
    shapes = [
        (WIDTH, WIDTH), (WIDTH, WIDTH), (2 * WIDTH, WIDTH), (WIDTH, WIDTH),
        (3 * WIDTH, WIDTH), (WIDTH, WIDTH), (2 * WIDTH, WIDTH), (WIDTH, WIDTH),
        (PLANE, 128, WIDTH), (PLANE, 128, WIDTH),
    ]
    return pl.pallas_call(
        layer_kernel,
        in_specs=[pl.BlockSpec(memory_space=pltpu.VMEM)] * len(operands),
        out_specs=[pl.BlockSpec(memory_space=pltpu.VMEM)] * 2,
        out_shape=[
            jax.ShapeDtypeStruct((NODES, ROWS), BF16),
            jax.ShapeDtypeStruct((1024, WIDTH), BF16),
        ],
        scratch_shapes=[pltpu.VMEM(shape, BF16) for shape in shapes]
        + [
            pltpu.VMEM((PLANE, 2, 128), jnp.int32),
            pltpu.VMEM((2 * NODES, WIDTH), F32),
            pltpu.VMEM((2 * NODES, WIDTH), BF16),
            pltpu.VMEM((DEPTH, NODES, WIDTH), BF16),
            pltpu.VMEM((LON, ROWS, WIDTH), BF16),
            pltpu.VMEM((ROWS, WIDTH), BF16),
            pltpu.VMEM((ROWS, WIDTH), BF16),
            pltpu.VMEM((ROWS, WIDTH), BF16),
            pltpu.VMEM((NODES, WIDTH), BF16),
            pltpu.VMEM((LAT, 8, WIDTH), BF16),
            pltpu.VMEM((LAT, 8, WIDTH), BF16),
            pltpu.VMEM((1024, WIDTH), F32),
            pltpu.VMEM((NODES, WIDTH), F32),
            pltpu.VMEM((ROWS, WIDTH), BF16),
            pltpu.VMEM((NODES, ROWS), BF16),
            dma((2, PLANE)), dma((2, PLANE)), dma((PLANE,)), dma((PLANE,)),
            dma((2, LON + 1)), dma((DEPTH, LON + 1)), dma((LON,)), dma((1,)),
            dma((LON,)), dma((LON,)), dma((LON,)), dma((LON,)),
            dma((LAT,)), dma((LAT,)), dma((LON,)), dma((LON,)), dma((LON,)), dma((LON,)),
            dma((8,)), dma((8,)), dma((8,)), dma((8,)), dma((8,)), dma((8,)),
        ],
        compiler_params=pltpu.CompilerParams(
            collective_id=0, has_side_effects=True, vmem_limit_bytes=60 * 1024 * 1024
        ),
        name="layer",
    )(*operands)


def local(
    grid_latent,
    grid_feat,
    grid_sender,
    grid_owner,
    grid_node,
    mesh_latent,
    mesh_edge,
    halo_send,
    mesh_sender,
    mesh_receiver,
    enc_edge_in,
    enc_feat_proj,
    enc_edge_out,
    enc_edge_bias,
    enc_edge_gain,
    enc_node_in,
    enc_node_out,
    enc_node_bias,
    enc_node_gain,
    proc_edge_in,
    proc_edge_out,
    proc_edge_bias,
    proc_edge_gain,
    proc_node_in,
    proc_node_out,
    proc_node_bias,
    proc_node_gain,
):
    idx, fields = slots(
        grid_owner.reshape(1, -1), grid_sender.reshape(1, -1), grid_node.reshape(1, -1), grid_feat
    )
    proj = jnp.concatenate([enc_feat_proj, jnp.zeros((4, WIDTH), BF16)], 0)
    return layer(
        idx.reshape(PLANE, 2, 128),
        fields.reshape(PLANE, 8, 128),
        grid_latent,
        mesh_latent,
        halo_send.reshape(1, -1),
        mesh_edge,
        mesh_sender.reshape(4, 1, 256),
        mesh_receiver.reshape(4, 1, 256),
        proj,
        enc_edge_bias,
        enc_edge_gain[None],
        enc_node_bias,
        enc_node_gain[None],
        proc_edge_bias,
        proc_edge_gain[None],
        proc_node_bias,
        proc_node_gain[None],
        enc_edge_in,
        enc_edge_out,
        enc_node_in,
        enc_node_out,
        proc_edge_in,
        proc_edge_out,
        proc_node_in,
        proc_node_out,
    )


def solution(mesh):
    placed = (
        P(("lat", "lon"), None),
        P(None, ("lat", "lon")),
        P(("lat", "lon")),
        P(("lat", "lon"), None),
        P(("lat", "lon")),
        P("lat", "lon"),
        P(("lat", "lon"), None),
        P("lat", None),
        P(("lat", "lon")),
        P(("lat", "lon")),
        P(None, "lon"),
        P(),
        P(None, "lon"),
        P(),
        P(),
        P(None, "lon"),
        P("lon", None),
        P(),
        P(),
        P(None, "lon"),
        P(None, "lon"),
        P(),
        P(),
        P(None, "lon"),
        P("lon", None),
        P(),
        P(),
    )
    return jax.shard_map(
        local,
        mesh=mesh,
        in_specs=placed,
        out_specs=(P("lat", "lon"), P(("lat", "lon"), None)),
        check_vma=False,
    )
```

```python
import jax
import jax.numpy as jnp
from jax import lax
from jax.experimental import pallas as pl
from jax.experimental.pallas import tpu as pltpu
from jax.sharding import PartitionSpec as P

F32 = jnp.float32
BF16 = jnp.bfloat16
LAT = 64
LON = 4
WIDTH = 512
NODES = 512
CAP = 64
ROWS = NODES // LON
PLANE = 32
DEPTH = 8
HALF = WIDTH // 2
MESH = pl.DeviceIdType.MESH


def matmul(a, b):
    return jnp.dot(a, b, preferred_element_type=F32)


def matmul_t(a, b):
    return lax.dot_general(a, b, (((0,), (0,)), ((), ())), preferred_element_type=F32)


def matmul_nt(a, b):
    return lax.dot_general(a, b, (((1,), (1,)), ((), ())), preferred_element_type=F32)


def swish(t):
    return t / (1.0 + jnp.exp(-t))


def layer_norm(values, gain, offset):
    average = jnp.mean(values, axis=-1, keepdims=True)
    centred = values - average
    spread = jnp.mean(centred * centred, axis=-1, keepdims=True)
    return centred * lax.rsqrt(spread + 1e-05) * gain + offset


def one_hot(row, count):
    width = row.shape[1]
    return (lax.broadcasted_iota(jnp.int32, (count, width), 0) == row).astype(BF16)


def fill_slots(owner, sender, node, feat, idx, fields):
    count = owner.shape[1]
    block = 128
    owners = owner[...]
    hit = one_hot(owners, LAT)
    row = lax.broadcasted_iota(jnp.int32, (block, block), 0)
    column = lax.broadcasted_iota(jnp.int32, (block, block), 1)
    above = (row < column).astype(BF16)
    carry = jnp.zeros((LAT, 1), F32)
    ranks = []
    for at in range(0, count, block):
        part = hit[:, at : at + block]
        wide = part.astype(F32)
        before = matmul(part, above) + carry
        ranks.append(jnp.sum(before * wide, axis=0, keepdims=True))
        carry = carry + jnp.sum(wide, axis=1, keepdims=True)
    rank = jnp.concatenate(ranks, axis=1).astype(jnp.int32)
    half = owners // 32
    target = (owners % 8) * 4 + (owners // 8) % 2 * 2 + (owners // 16) % 2
    at_target = one_hot(target, PLANE)
    place = one_hot(rank + half * CAP, 2 * CAP).astype(F32)
    named = node[...] + half * NODES + 1

    def put(values):
        return matmul_nt(at_target, (place * values.astype(F32)).astype(BF16))

    def put_whole(values):
        return (put(values // 32) * 32.0 + put(values % 32)).astype(jnp.int32)

    rows = [put_whole(sender[...]), put_whole(named) - 1]
    for t in range(PLANE):
        for i in range(2):
            idx[t, i : i + 1, :] = rows[i][t : t + 1, :]
    fields[...] = jnp.zeros_like(fields)
    for i in range(4):
        features = put(feat[i : i + 1, :])
        for t in range(PLANE):
            fields[t, i : i + 1, :] = features[t : t + 1, :]


def remote(source, target, send, receive, where):
    return pltpu.make_async_remote_copy(
        src_ref=source,
        dst_ref=target,
        send_sem=send,
        recv_sem=receive,
        device_id=where,
        device_id_type=MESH,
    )


AROUND = (False, True, False, True, False, True, True, True)
COLUMNS = (True, True, True, False, True, True, True, False)


def layer_kernel(
    g_owner, g_sender, g_node, g_feat, grid, mesh, halo_rows, edges, sender, receiver, proj,
    edge_bias, edge_gain, node_bias, node_gain, proc_bias, proc_gain, last_bias, last_gain,
    k0, k1, k2, k3, k4, k5, k6, k7,
    out, edge_out,
    w0, w1, w2, w3, w4, w5, w6, w7,
    send, got, got_ids, idx, feat, acc, part, plane, share, aggregate, base, middle, whole,
    outgoing, halo, pre_all, incoming, newest, update,
    s_msg, r_msg, s_ids, r_ids, s_z, r_z, s_share, r_share, s_base, r_base, s_mid, r_mid,
    s_halo, r_halo, s_inc, r_inc, s_new, r_new,
    s_part, r_part, s_cross, r_cross, s_fwd, r_fwd,
):
    pieces = (k0, k1, k2, k3, k4, k5, k6, k7)
    weights = (w0, w1, w2, w3, w4, w5, w6, w7)
    lat = lax.axis_index("lat")
    lon = lax.axis_index("lon")
    z = lat // 8
    cell = lat % 8
    place = cell * LON + lon
    shelf = 2 * (lon % 2) + lon // 2
    owner = z % 4 == shelf

    def at_place(t):
        return {"lat": z * 8 + t // LON, "lon": t % LON}

    def at_depth(depth):
        return {"lat": depth * 8 + cell, "lon": lon}

    def at_lon(other):
        return {"lat": lat, "lon": other}

    def beside(step):
        return at_lon((lon + step) % LON)

    def behind(step):
        return (lon - step + LON) % LON

    def rows_of(q):
        return pl.ds(pl.multiple_of(q * ROWS, ROWS), ROWS)

    mine = rows_of(lon)
    barrier = pltpu.get_barrier_semaphore()

    def greet(d, _):
        pl.semaphore_signal(
            barrier, inc=1, device_id={"lat": (lat + d) % LAT, "lon": lon}, device_id_type=MESH
        )
        return 0

    lax.fori_loop(1, LAT, greet, 0)
    for step in range(1, LON):

        def greet_plane(c, _):
            pl.semaphore_signal(
                barrier,
                inc=1,
                device_id={"lat": z * 8 + (cell + c) % 8, "lon": (lon + step) % LON},
                device_id_type=MESH,
            )
            return 0

        lax.fori_loop(0, 8, greet_plane, 0)

    def target(d):
        turn = (d * 13) % PLANE
        row = (place // 8 + turn // 8) % 4
        column = (place // 2 + turn // 2) % 4
        return row * 8 + column * 2 + (place + turn) % 2

    def pick(s, _):
        one, two = target(2 * s), target(2 * s + 1)
        names = jnp.concatenate([idx[one][0:1, :], idx[two][0:1, :]], axis=1)
        rows = matmul_t(one_hot(names, WIDTH), grid[...]).astype(BF16)
        send[2 * s] = rows[:128]
        send[2 * s + 1] = rows[128:]
        return 0

    def compute(d):
        one, two = target(d), target(d + 1)
        features = jnp.concatenate([feat[one], feat[two]], axis=1).astype(BF16)
        rows = jnp.concatenate([send[d], send[d + 1]], axis=0)
        pre = matmul(rows, w0[...]) + (matmul_t(features, proj[...]) + edge_bias[0:1, :])
        raw = matmul_nt(swish(pre).astype(BF16), w1[...])
        message = layer_norm(raw, edge_gain[...], edge_bias[1:2, :]).astype(BF16)
        send[d] = message[:128]
        send[d + 1] = message[128:]

    def message_copy(d, half):
        columns = pl.ds(half * HALF, HALF)
        return remote(
            send.at[d, :, columns],
            got.at[d, :, columns],
            s_msg.at[half, d],
            r_msg.at[half, d],
            at_place(target(d)),
        )

    def ids_copy(d):
        return remote(idx.at[target(d)], got_ids.at[d], s_ids.at[d], r_ids.at[d], at_place(target(d)))

    def base_copy(step, writer):
        return remote(
            mesh.at[rows_of((lon + step) % LON), :],
            base.at[:, rows_of(writer)],
            s_base.at[step],
            r_base.at[step],
            beside(step),
        )

    partner = lon + 1 - 2 * (lon % 2)
    cross = (lon + 2) % LON
    corner = partner + 2 - 4 * (partner // 2)

    def block(i, q):
        return weights[i].at[:, rows_of(q)] if COLUMNS[i] else weights[i].at[rows_of(q), :]

    def to_partner(i, q):
        return remote(pieces[i], block(i, q), s_part.at[i], r_part.at[i], at_lon(partner))

    def to_cross(i, q):
        where = {"lat": lat + 1 - 2 * (lat % 2), "lon": cross} if AROUND[i] else at_lon(cross)
        return remote(pieces[i], block(i, q), s_cross.at[i], r_cross.at[i], where)

    def forward(i, q):
        return remote(block(i, q), block(i, q), s_fwd.at[i], r_fwd.at[i], at_lon(partner))

    def offer(i):
        to_cross(i, lon).start()
        to_partner(i, lon).start()

    def relay(i):
        to_cross(i, cross).wait_recv()
        forward(i, cross).start()

    def settle(i):
        to_partner(i, partner).wait_recv()
        forward(i, corner).wait_recv()

    fill_slots(g_owner, g_sender, g_node, g_feat, idx, feat)
    lax.fori_loop(0, 4, pick, 0)
    pl.semaphore_wait(barrier, LAT - 1 + 24)
    offer(0)
    offer(1)

    def start_ids(d, _):
        ids_copy(d).start()
        return 0

    lax.fori_loop(1, PLANE, start_ids, 0)
    for step in range(1, LON):
        base_copy(step, lon).start()
    for i in range(8):
        if COLUMNS[i]:
            weights[i][:, mine] = pieces[i][...]
        else:
            weights[i][mine, :] = pieces[i][...]
    base[:, mine] = mesh[mine, :]
    lax.fori_loop(4, PLANE // 2, pick, 0)
    relay(0)
    relay(1)
    settle(0)
    settle(1)

    compute(0)
    got[0] = send[0]
    got_ids[0] = idx[place]
    message_copy(1, 0).start()

    def start_messages(s, _):
        compute(2 * s)
        message_copy(2 * s, 0).start()
        message_copy(2 * s + 1, 0).start()
        return 0

    lax.fori_loop(1, PLANE // 2, start_messages, 0)

    offer(2)
    offer(3)

    def start_rest(d, _):
        message_copy(d, 1).start()
        return 0

    lax.fori_loop(1, PLANE, start_rest, 0)

    acc[...] = jnp.zeros_like(acc)

    def take(g, half):
        columns = slice(half * HALF, (half + 1) * HALF)
        ids = jnp.concatenate([got_ids[4 * g + i][1:2, :] for i in range(4)], axis=1)
        rows = jnp.concatenate([got[4 * g + i, :, columns] for i in range(4)], axis=0)
        acc[:, columns] += matmul(one_hot(ids, 2 * NODES), rows)

    def arrive(d, half):
        if half == 0:
            ids_copy(d).wait_recv()
        message_copy(d, half).wait_recv()

    def collect(half):
        for d in range(1, 4):
            arrive(d, half)
        take(0, half)

        def group(g, _):
            for i in range(4):
                arrive(4 * g + i, half)
            take(g, half)
            return 0

        lax.fori_loop(1, PLANE // 4, group, 0)

    def depth_copy(j, q):
        depth = shelf + 4 * j
        away = (depth - z + DEPTH) % DEPTH
        if q == LON:
            source = part.at[pl.ds(j * NODES, NODES), pl.ds(0, HALF)]
            goal = plane.at[away, :, pl.ds(0, HALF)]
        else:
            source = part.at[pl.ds(j * NODES + q * ROWS, ROWS), pl.ds(HALF, HALF)]
            goal = plane.at[away, pl.ds(q * ROWS, ROWS), pl.ds(HALF, HALF)]
        return remote(source, goal, s_z.at[j, q], r_z.at[away, q], at_depth(depth))

    collect(0)
    part[:, :HALF] = acc[:, :HALF].astype(BF16)
    for j in range(2):

        @pl.when(z != shelf + 4 * j)
        def _():
            depth_copy(j, LON).start()

    collect(1)
    for q in range(LON):
        for j in range(2):
            rows = pl.ds(j * NODES + q * ROWS, ROWS)
            part[rows, HALF:] = acc[rows, HALF:].astype(BF16)

            @pl.when(z != shelf + 4 * j)
            def _():
                depth_copy(j, q).start()

    for i in range(4, 8):
        offer(i)
    relay(2)
    relay(3)

    def share_copy(q):
        return remote(share.at[q], aggregate, s_share.at[q], r_share.at[0], at_lon(q))

    def depth_arrival(away, q):
        if q == LON:
            source = part.at[pl.ds(0, NODES), pl.ds(0, HALF)]
            goal = plane.at[away, :, pl.ds(0, HALF)]
        else:
            source = part.at[pl.ds(0, ROWS), pl.ds(HALF, HALF)]
            goal = plane.at[away, pl.ds(q * ROWS, ROWS), pl.ds(HALF, HALF)]
        return remote(source, goal, s_z.at[0, q], r_z.at[away, q], at_depth(z))

    @pl.when(owner)
    def _():
        for away in range(1, DEPTH):
            depth_arrival(away, LON).wait_recv()
        for q in range(LON):
            first = pl.multiple_of((z // 4) * NODES + q * ROWS, ROWS)
            total = acc[pl.ds(first, ROWS), :]
            for away in range(1, DEPTH):
                depth_arrival(away, q).wait_recv()
                total = total + plane[away, pl.ds(q * ROWS, ROWS), :].astype(F32)
            rounded = total.astype(BF16)

            @pl.when(lon == q)
            def _():
                aggregate[...] = rounded

            @pl.when(lon != q)
            def _():
                share[q] = rounded
                share_copy(q).start()

    settle(2)
    settle(3)
    for step in range(1, LON):
        base_copy(step, behind(step)).wait_recv()

    def node_network(before, pre_base, summed, w_in, w_out, bias, gain):
        pre = pre_base + matmul(summed, w_in[WIDTH:, :]) + bias[0:1, :]
        raw = matmul(swish(pre).astype(BF16), w_out[...])
        return (before.astype(F32) + layer_norm(raw, gain[...], bias[1:2, :])).astype(BF16)

    pre_base = matmul(base[...], w2[:WIDTH, :])

    @pl.when(z % 4 != shelf)
    def _():
        share_copy(0).wait_recv()

    middle[...] = node_network(base[...], pre_base, aggregate[...], w2, w3, node_bias, node_gain)

    def middle_copy(step, writer):
        return remote(middle, whole.at[rows_of(writer), :], s_mid.at[step], r_mid.at[step], beside(step))

    for step in range(1, LON):
        middle_copy(step, lon).start()
    whole[mine, :] = middle[...]
    for i in range(4, 8):
        relay(i)
    for step in range(1, LON):
        middle_copy(step, behind(step)).wait_recv()

    chosen = matmul_t(one_hot(halo_rows[...], NODES), whole[...])
    outgoing[...] = chosen.reshape(LAT, 8, WIDTH).astype(BF16)

    def halo_copy(d, writer):
        other = (lat + d) % LAT
        return remote(
            outgoing.at[other], halo.at[writer], s_halo.at[d], r_halo.at[d], {"lat": other, "lon": lon}
        )

    def start_halo(d, _):
        halo_copy(d, lat).start()
        return 0

    lax.fori_loop(1, LAT, start_halo, 0)
    halo[lat] = outgoing[lat]
    for i in range(4, 8):
        settle(i)

    def begin(c, _):
        rows = pl.ds(pl.multiple_of(c * 256, 256), 256)
        sent = matmul_t(one_hot(sender[c], NODES), whole[...]).astype(BF16)
        received = matmul_t(one_hot(receiver[c], NODES), whole[...]).astype(BF16)
        pre = matmul(edges[rows, :], w4[:WIDTH, :])
        pre = pre + matmul(sent, w4[WIDTH : 2 * WIDTH, :])
        pre = pre + matmul(received, w4[2 * WIDTH :, :])
        pre_all[rows, :] = pre + proc_bias[0:1, :]
        return 0

    lax.fori_loop(0, 4, begin, 0)
    last_base = matmul(middle[...], w6[:WIDTH, :])

    def end_halo(d, _):
        halo_copy(d, (lat - d + LAT) % LAT).wait_recv()
        return 0

    lax.fori_loop(1, LAT, end_halo, 0)
    incoming[...] = jnp.zeros_like(incoming)
    table = halo[...].astype(F32).reshape(NODES, WIDTH).astype(BF16)

    def finish(c, _):
        rows = pl.ds(pl.multiple_of(c * 256, 256), 256)
        sent = matmul_t(one_hot(sender[c] - NODES, NODES), table).astype(BF16)
        pre = pre_all[rows, :] + matmul(sent, w4[WIDTH : 2 * WIDTH, :])
        raw = matmul_nt(swish(pre).astype(BF16), w5[...])
        old = edges[rows, :].astype(F32)
        updated = (old + layer_norm(raw, proc_gain[...], proc_bias[1:2, :])).astype(BF16)
        edge_out[rows, :] = updated
        incoming[...] += matmul(one_hot(receiver[c], NODES), updated)
        return 0

    lax.fori_loop(0, 4, finish, 0)
    for q in range(LON + 1):
        for j in range(2):

            @pl.when(z != shelf + 4 * j)
            def _():
                depth_copy(j, q).wait_send()

    for q in range(LON):
        share_rows = pl.ds(q * ROWS, ROWS)
        part[share_rows, :] = incoming[share_rows, :].astype(BF16)

    def incoming_copy(step):
        return remote(
            part.at[rows_of((lon + step) % LON), :],
            plane.at[0, pl.ds(step * ROWS, ROWS), :],
            s_inc.at[step],
            r_inc.at[step],
            beside(step),
        )

    for step in range(1, LON):
        incoming_copy(step).start()
    total = incoming[mine, :]
    for step in range(1, LON):
        incoming_copy(step).wait_recv()
        total = total + plane[0, step * ROWS : (step + 1) * ROWS, :].astype(F32)
    newest[...] = node_network(middle[...], last_base, total.astype(BF16), w6, w7, last_bias, last_gain)

    def newest_copy(step, writer):
        return remote(
            newest.at[:, rows_of((lon + step) % LON)],
            update.at[rows_of(writer), :],
            s_new.at[step],
            r_new.at[step],
            beside(step),
        )

    for step in range(1, LON):
        newest_copy(step, lon).start()
    update[mine, :] = newest[:, mine]

    def sent(d, _):
        ids_copy(d).wait_send()
        message_copy(d, 0).wait_send()
        message_copy(d, 1).wait_send()
        return 0

    lax.fori_loop(1, PLANE, sent, 0)

    def sent_halo(d, _):
        halo_copy(d, lat).wait_send()
        return 0

    lax.fori_loop(1, LAT, sent_halo, 0)
    for i in range(8):
        to_cross(i, lon).wait_send()
        to_partner(i, lon).wait_send()
        forward(i, cross).wait_send()
    for step in range(1, LON):
        base_copy(step, lon).wait_send()
        middle_copy(step, lon).wait_send()
        incoming_copy(step).wait_send()
        newest_copy(step, lon).wait_send()

    @pl.when(owner)
    def _():
        for q in range(LON):

            @pl.when(lon != q)
            def _():
                share_copy(q).wait_send()

    for step in range(1, LON):
        newest_copy(step, behind(step)).wait_recv()
    out[...] = update[...]


def layer(*operands):
    dma = pltpu.SemaphoreType.DMA
    shapes = [
        (WIDTH, WIDTH), (WIDTH, WIDTH), (2 * WIDTH, WIDTH), (WIDTH, WIDTH),
        (3 * WIDTH, WIDTH), (WIDTH, WIDTH), (2 * WIDTH, WIDTH), (WIDTH, WIDTH),
        (PLANE, 128, WIDTH), (PLANE, 128, WIDTH),
    ]
    return pl.pallas_call(
        layer_kernel,
        in_specs=[pl.BlockSpec(memory_space=pltpu.VMEM)] * len(operands),
        out_specs=[pl.BlockSpec(memory_space=pltpu.VMEM)] * 2,
        out_shape=[
            jax.ShapeDtypeStruct((NODES, ROWS), BF16),
            jax.ShapeDtypeStruct((1024, WIDTH), BF16),
        ],
        scratch_shapes=[pltpu.VMEM(shape, BF16) for shape in shapes]
        + [
            pltpu.VMEM((PLANE, 2, 128), jnp.int32),
            pltpu.VMEM((PLANE, 2, 128), jnp.int32),
            pltpu.VMEM((PLANE, 8, 128), F32),
            pltpu.VMEM((2 * NODES, WIDTH), F32),
            pltpu.VMEM((2 * NODES, WIDTH), BF16),
            pltpu.VMEM((DEPTH, NODES, WIDTH), BF16),
            pltpu.VMEM((LON, ROWS, WIDTH), BF16),
            pltpu.VMEM((ROWS, WIDTH), BF16),
            pltpu.VMEM((ROWS, WIDTH), BF16),
            pltpu.VMEM((ROWS, WIDTH), BF16),
            pltpu.VMEM((NODES, WIDTH), BF16),
            pltpu.VMEM((LAT, 8, WIDTH), BF16),
            pltpu.VMEM((LAT, 8, WIDTH), BF16),
            pltpu.VMEM((1024, WIDTH), F32),
            pltpu.VMEM((NODES, WIDTH), F32),
            pltpu.VMEM((ROWS, WIDTH), BF16),
            pltpu.VMEM((NODES, ROWS), BF16),
            dma((2, PLANE)), dma((2, PLANE)), dma((PLANE,)), dma((PLANE,)),
            dma((2, LON + 1)), dma((DEPTH, LON + 1)), dma((LON,)), dma((1,)),
            dma((LON,)), dma((LON,)), dma((LON,)), dma((LON,)),
            dma((LAT,)), dma((LAT,)), dma((LON,)), dma((LON,)), dma((LON,)), dma((LON,)),
            dma((8,)), dma((8,)), dma((8,)), dma((8,)), dma((8,)), dma((8,)),
        ],
        compiler_params=pltpu.CompilerParams(
            collective_id=0, has_side_effects=True, vmem_limit_bytes=60 * 1024 * 1024
        ),
        name="layer",
    )(*operands)


def local(
    grid_latent,
    grid_feat,
    grid_sender,
    grid_owner,
    grid_node,
    mesh_latent,
    mesh_edge,
    halo_send,
    mesh_sender,
    mesh_receiver,
    enc_edge_in,
    enc_feat_proj,
    enc_edge_out,
    enc_edge_bias,
    enc_edge_gain,
    enc_node_in,
    enc_node_out,
    enc_node_bias,
    enc_node_gain,
    proc_edge_in,
    proc_edge_out,
    proc_edge_bias,
    proc_edge_gain,
    proc_node_in,
    proc_node_out,
    proc_node_bias,
    proc_node_gain,
):
    proj = jnp.concatenate([enc_feat_proj, jnp.zeros((4, WIDTH), BF16)], 0)
    return layer(
        grid_owner.reshape(1, -1),
        grid_sender.reshape(1, -1),
        grid_node.reshape(1, -1),
        grid_feat,
        grid_latent,
        mesh_latent,
        halo_send.reshape(1, -1),
        mesh_edge,
        mesh_sender.reshape(4, 1, 256),
        mesh_receiver.reshape(4, 1, 256),
        proj,
        enc_edge_bias,
        enc_edge_gain[None],
        enc_node_bias,
        enc_node_gain[None],
        proc_edge_bias,
        proc_edge_gain[None],
        proc_node_bias,
        proc_node_gain[None],
        enc_edge_in,
        enc_edge_out,
        enc_node_in,
        enc_node_out,
        proc_edge_in,
        proc_edge_out,
        proc_node_in,
        proc_node_out,
    )


def solution(mesh):
    placed = (
        P(("lat", "lon"), None),
        P(None, ("lat", "lon")),
        P(("lat", "lon")),
        P(("lat", "lon"), None),
        P(("lat", "lon")),
        P("lat", "lon"),
        P(("lat", "lon"), None),
        P("lat", None),
        P(("lat", "lon")),
        P(("lat", "lon")),
        P(None, "lon"),
        P(),
        P(None, "lon"),
        P(),
        P(),
        P(None, "lon"),
        P("lon", None),
        P(),
        P(),
        P(None, "lon"),
        P(None, "lon"),
        P(),
        P(),
        P(None, "lon"),
        P("lon", None),
        P(),
        P(),
    )
    return jax.shard_map(
        local,
        mesh=mesh,
        in_specs=placed,
        out_specs=(P("lat", "lon"), P(("lat", "lon"), None)),
        check_vma=False,
    )
```
